256 devices in a mesh: pipe: 2 (over core), obs: 16 (over y, x), patch: 8 (over z).
Axes of the slice: x: 4, y: 4, z: 8, core: 2. Of those that a mesh axis runs over, the one named last changes fastest.
Arguments:
- patch_tokens: bfloat16 [4096, 2048], P('patch', 'obs'), may hold values from -40 to 40
- obs_tokens: bfloat16 [2048, 2048], P('patch', 'obs'), may hold values from -40 to 40
- footprint: int32 [32, 8], P('patch'), may hold values from 0 to 15, as said below
- list_counts: int32 [32], P('patch'), may hold values from 1 to 8
- footprint_bias: float32 [32, 8], P('patch'), may hold values from -4 to 290
- w_query: bfloat16 [2, 2048, 2048], P('pipe', None, 'obs'), may hold values from -0.125 to 0.125
- w_key: bfloat16 [2, 2048, 2048], P('pipe', None, 'obs'), may hold values from -0.125 to 0.125
- w_value: bfloat16 [2, 2048, 2048], P('pipe', None, 'obs'), may hold values from -0.125 to 0.125
- w_out: bfloat16 [2, 2048, 2048], P('pipe', 'obs'), may hold values from -0.125 to 0.125
- patch_gain: float32 [2, 2048], P('pipe'), may hold values from 0.1 to 1.9
- obs_gain: float32 [2, 2048], P('pipe'), may hold values from 0.1 to 1.9
Outputs:
- sections: bfloat16 [2, 4096, 2048], P('pipe', 'patch', 'obs')
The draws below stay inside these ranges and needn't reach their ends.
Inputs may be any that keep to these rules, and one draw needn't show every extreme that they name: `footprint`: entries are global observation block indices. In each row the first list_counts entries (the live ones) are distinct, the rest are to be ignored. For a device along patch and any device along patch, all live entries of the first device's rows that lie in the second device's range of 2 blocks name one and the same block.
All inputs are finite; a program needn't handle non-finite values.
Results may differ from the reference program's by a relative error of at most 0.012.
Values may be sent and summed in bfloat16 or wider, within the bound.
No kernel may reach another device: no remote copies, remote signals or barrier semaphores. Data moves between devices by JAX's collectives and lax.ppermute only.
A program may use at most 64 MiB of HBM per device.

```python
import math
import jax
import jax.numpy as jnp
from jax import lax

D = 2048
HEADS = 16
HS = 128
BLK = 128
SEGMENTS = 2
GROUPS = 16
MAXL = 8
P_SIZE = 4096
NOBS = 2048
PBLK = 32
NOBLK = 16
PBLK_DEV = 4
OBLK_DEV = 2


def token_field(key, row_count, col_count):
    base_field = jax.random.truncated_normal(jax.random.fold_in(key, 1), -4.0, 4.0, (row_count, col_count), jnp.float32)
    row_scale = jnp.exp(jax.random.uniform(jax.random.fold_in(key, 2), (row_count, 1), jnp.float32, math.log(0.3), math.log(3.0)))
    col_scale = jnp.exp(jax.random.uniform(jax.random.fold_in(key, 3), (1, col_count), jnp.float32, math.log(0.5), math.log(2.0)))
    return (base_field * row_scale * col_scale).astype(jnp.bfloat16)


def draw_patch_tokens(key, part):
    return token_field(jax.random.fold_in(key, 101), P_SIZE, D)


def draw_obs_tokens(key, part):
    return token_field(jax.random.fold_in(key, 202), NOBS, D)


def footprint_parts(key):
    device_count = PBLK // PBLK_DEV
    picked = jax.random.randint(jax.random.fold_in(key, 11), (device_count, device_count), 0, OBLK_DEV)
    block_keys = jax.random.split(jax.random.fold_in(key, 12), PBLK)
    orders = jax.vmap(lambda one_key: jax.random.permutation(one_key, device_count))(block_keys)
    chosen = orders[:, :MAXL].astype(jnp.int32)
    owners = (jnp.arange(PBLK) // PBLK_DEV).astype(jnp.int32)
    entries = chosen * OBLK_DEV + picked[owners[:, None], chosen]
    counts = jax.random.randint(jax.random.fold_in(key, 13), (PBLK,), 1, MAXL + 1)
    full_at = jax.random.randint(jax.random.fold_in(key, 14), (), 0, PBLK)
    counts = jnp.where(jnp.arange(PBLK) == full_at, MAXL, counts)
    return (entries.astype(jnp.int32), counts.astype(jnp.int32))


def draw_footprint(key, part):
    entries, counts = footprint_parts(jax.random.fold_in(key, 303))
    return entries


def draw_list_counts(key, part):
    entries, counts = footprint_parts(jax.random.fold_in(key, 303))
    return counts


def draw_footprint_bias(key, part):
    values = jax.random.uniform(jax.random.fold_in(key, 32), (PBLK, MAXL), jnp.float32, -2.0, 2.0)
    return values


def level_of(own_key, shape, cuts, low, top_value):
    loudness = 1.0
    for position, shards_of in cuts:
        steps = jax.random.uniform(jax.random.fold_in(jax.random.fold_in(own_key, 6), position), (shards_of,), jnp.float32, low / len(cuts), top_value / len(cuts))
        loudness = loudness * jnp.repeat(jnp.exp(steps), shape[position] // shards_of).reshape((-1,) + (1,) * (len(shape) - 1 - position))
    return loudness


def centred(stream_key, shape, scale, bound, shards=(), dtype=jnp.bfloat16):
    values = scale * jax.random.normal(stream_key, shape, jnp.float32)
    if shards:
        values = values * level_of(stream_key, shape, shards, -0.22, 0.18)
    return jnp.clip(values, -bound, bound).astype(dtype)


def setup_inputs(seed: int = 0) -> dict:
    keys = jax.random.split(jax.random.key(seed), 12)
    patch_tokens = draw_patch_tokens(jax.random.fold_in(keys[11], 71), 0)
    obs_tokens = draw_obs_tokens(jax.random.fold_in(keys[11], 71), 0)
    footprint = draw_footprint(jax.random.fold_in(keys[11], 71), 0)
    list_counts = draw_list_counts(jax.random.fold_in(keys[11], 71), 0)
    footprint_bias = draw_footprint_bias(jax.random.fold_in(keys[11], 71), 0)
    w_query = centred(keys[5], (SEGMENTS, D, HEADS * HS), D ** -0.5, 0.125, ((0, 2), (2, 16)))
    w_key = centred(keys[6], (SEGMENTS, D, HEADS * HS), D ** -0.5, 0.125, ((0, 2), (2, 16)))
    w_value = centred(keys[7], (SEGMENTS, D, HEADS * HS), D ** -0.5, 0.125, ((0, 2), (2, 16)))
    w_out = centred(keys[8], (SEGMENTS, HEADS * HS, D), (HEADS * HS) ** -0.5, 0.125, ((0, 2), (1, 16)))
    patch_gain = jnp.clip(1.0 + 0.18 * jax.random.normal(keys[9], (SEGMENTS, D), jnp.float32), 0.1, 1.9)
    obs_gain = jnp.clip(1.0 + 0.18 * jax.random.normal(keys[10], (SEGMENTS, D), jnp.float32), 0.1, 1.9)
    return dict(patch_tokens=patch_tokens, obs_tokens=obs_tokens, footprint=footprint, list_counts=list_counts, footprint_bias=footprint_bias, w_query=w_query, w_key=w_key, w_value=w_value, w_out=w_out, patch_gain=patch_gain, obs_gain=obs_gain)


def rms_round(values, gain):
    widened = values.astype(jnp.float32)
    scaled = widened * lax.rsqrt(lax.optimization_barrier(jnp.mean(widened * widened, axis=-1, keepdims=True)) + 1e-05)
    return (scaled * gain.astype(jnp.float32)).astype(jnp.bfloat16)

def reference(patch_tokens, obs_tokens, footprint, list_counts, footprint_bias, w_query, w_key, w_value, w_out, patch_gain, obs_gain):
    full_width = HEADS * HS
    group_width = full_width // GROUPS
    current = patch_tokens
    results = []
    for section in range(SEGMENTS):
        obs_normed = rms_round(obs_tokens, obs_gain[section])
        key_rows = jnp.dot(obs_normed, w_key[section], preferred_element_type=jnp.float32).astype(jnp.bfloat16)
        value_rows = jnp.dot(obs_normed, w_value[section], preferred_element_type=jnp.float32).astype(jnp.bfloat16)
        key_rows = lax.optimization_barrier(key_rows).reshape(NOBLK, BLK, HEADS, HS)
        value_rows = lax.optimization_barrier(value_rows).reshape(NOBLK, BLK, HEADS, HS)
        patch_normed = rms_round(current, patch_gain[section])
        queries = (jnp.dot(patch_normed, w_query[section], preferred_element_type=jnp.float32) * HS ** (-0.5)).astype(jnp.bfloat16)
        queries = lax.optimization_barrier(queries).reshape(PBLK, BLK, HEADS, HS)

        def one_block(items):
            query_block, listed, count_live, bias_row = items
            key_block = key_rows[listed].reshape(MAXL * BLK, HEADS, HS).astype(jnp.float32)
            value_block = value_rows[listed].reshape(MAXL * BLK, HEADS, HS).astype(jnp.float32)
            scores = jnp.einsum('qhd,khd->hqk', query_block.astype(jnp.float32), key_block)
            alive = jnp.repeat(jnp.arange(MAXL) < count_live, BLK)
            added = jnp.repeat(bias_row.astype(jnp.float32), BLK)
            scores = jnp.where(alive[None, None, :], scores + added[None, None, :], -1e+30)
            row_max = lax.optimization_barrier(jnp.max(scores, axis=-1, keepdims=True))
            weights = jnp.exp(scores - row_max)
            weights = (weights / lax.optimization_barrier(jnp.sum(weights, axis=-1, keepdims=True))).astype(jnp.bfloat16)
            weights = lax.optimization_barrier(weights).astype(jnp.float32)
            context = jnp.einsum('hqk,khd->qhd', weights, value_block).astype(jnp.bfloat16)
            return context.reshape(BLK, full_width)
        context = lax.map(one_block, (queries, footprint, list_counts, footprint_bias)).reshape(P_SIZE, full_width)
        head_total = jnp.zeros((P_SIZE, D), jnp.float32)
        for group in range(GROUPS):
            lower = group * group_width
            head_part = jnp.dot(context[:, lower:lower + group_width], w_out[section][lower:lower + group_width], preferred_element_type=jnp.float32).astype(jnp.bfloat16)
            head_part = lax.optimization_barrier(head_part)
            head_total = head_total + head_part.astype(jnp.float32)
        current = (current.astype(jnp.float32) + head_total).astype(jnp.bfloat16)
        results.append(current)
    return jnp.stack(results)
```

```python
import jax
import jax.numpy as jnp
from jax import lax
from jax.experimental import pallas as pl
from jax.experimental.pallas import tpu as pltpu
from jax.sharding import PartitionSpec as P

HS = 128
BLK = 128
SIDE = 4
EPS = 1e-05

SMEM = pl.BlockSpec(memory_space=pltpu.SMEM)
VMEM = pl.BlockSpec(memory_space=pltpu.VMEM)


def square_shift(first_axis, step):
    pairs = []
    for core in range(2):
        for row in range(SIDE):
            for col in range(SIDE):
                along_col = (core == 0) == first_axis
                new_row = row if along_col else (row + step) % SIDE
                new_col = (col + step) % SIDE if along_col else col
                base = core * SIDE * SIDE
                pairs.append((base + row * SIDE + col, base + new_row * SIDE + new_col))
    return pairs


def near(value, step):
    return lax.ppermute(value, ("pipe", "obs"), square_shift(True, step))


def far(value, step):
    return lax.ppermute(value, ("pipe", "obs"), square_shift(False, step))


def swapped(value):
    return lax.ppermute(value, "pipe", [(0, 1), (1, 0)])


def tile_cols(block):
    return pl.ds(pl.multiple_of(block * HS, HS), HS)


def normed_into(table, pieces, gain, normed):
    rows = normed.shape[0]
    squares = jnp.zeros((rows, HS), jnp.float32)
    for piece in pieces:
        for part in range(SIDE):
            widened = piece[part].astype(jnp.float32)
            squares = squares + widened * widened
    mean = jnp.sum(squares, axis=-1, keepdims=True) * (1.0 / (SIDE * SIDE * HS))
    inverse = lax.rsqrt(mean + EPS)
    for step, piece in enumerate(pieces):
        for part in range(SIDE):
            block = table[step * SIDE + part]
            scaled = (piece[part].astype(jnp.float32) * inverse) * gain[pl.ds(block, 1), :]
            normed[:, tile_cols(block)] = scaled.astype(jnp.bfloat16)


def key_value_kernel(table, o0, o1, o2, o3, gain, w_key, w_value, out, normed):
    normed_into(table, (o0, o1, o2, o3), gain, normed)
    for index, weight in enumerate((w_key, w_value)):
        out[:, index * HS : (index + 1) * HS] = jnp.dot(
            normed[...], weight[...], preferred_element_type=jnp.float32
        ).astype(jnp.bfloat16)


def attend_kernel(
    table,
    entries,
    counts,
    bias,
    x0,
    x1,
    x2,
    x3,
    kv_same,
    kv_other,
    gain,
    w_query,
    w_out,
    y0,
    y1,
    y2,
    y3,
    kept,
    normed,
    context,
):
    rows = normed.shape[0]
    slots = entries.shape[1]
    place, core, first_block = table[32], table[33], table[34]
    patch_count = kv_same.shape[0]
    normed_into(table, (x0, x1, x2, x3), gain, normed)
    for part in range(SIDE):
        kept[part] = x0[table[36 + part]]
    queries = (
        jnp.dot(normed[...], w_query[...], preferred_element_type=jnp.float32) * HS ** (-0.5)
    ).astype(jnp.bfloat16)
    for block in range(rows // BLK):
        query = queries[block * BLK : (block + 1) * BLK]
        row = first_block + block
        live = counts[row]
        scores, values = [], []
        for slot in range(slots):
            entry = jnp.where(slot < live, entries[row, slot], 0)
            owner = entry // 2
            index = lax.rem(place - owner + patch_count, patch_count)
            is_same = (entry - owner * 2) == core
            both = jnp.where(is_same, kv_same[index], kv_other[index])
            score = lax.dot_general(
                query,
                both[:, :HS],
                (((1,), (1,)), ((), ())),
                preferred_element_type=jnp.float32,
            )
            scores.append(jnp.where(slot < live, score + bias[row, slot], -1e30))
            values.append(both[:, HS:])
        scores = jnp.concatenate(scores, axis=1)
        top = jnp.max(scores, axis=-1, keepdims=True)
        weights = jnp.exp(scores - top)
        weights = (weights / jnp.sum(weights, axis=-1, keepdims=True)).astype(jnp.bfloat16)
        context[block * BLK : (block + 1) * BLK, :] = jnp.dot(
            weights, jnp.concatenate(values, axis=0), preferred_element_type=jnp.float32
        ).astype(jnp.bfloat16)
    ready = context[...]
    for step, out in enumerate((y0, y1, y2, y3)):
        for part in range(SIDE):
            block = table[16 + step * SIDE + part]
            out[part] = jnp.dot(
                ready, w_out[:, tile_cols(block)], preferred_element_type=jnp.float32
            ).astype(jnp.bfloat16)


def key_values(table, pieces, gain, w_key, w_value):
    rows = pieces[0].shape[1]
    features = w_key.shape[0]
    return pl.pallas_call(
        key_value_kernel,
        out_shape=jax.ShapeDtypeStruct((rows, 2 * HS), jnp.bfloat16),
        in_specs=[SMEM] + [VMEM] * 7,
        out_specs=VMEM,
        scratch_shapes=[pltpu.VMEM((rows, features), jnp.bfloat16)],
        cost_estimate=pl.CostEstimate(
            flops=4 * rows * features * HS, bytes_accessed=6 * features * HS, transcendentals=0
        ),
        name="key_values",
    )(table, *pieces, gain, w_key, w_value)


def attend(table, lists, pieces, kv_same, kv_other, gain, w_query, w_out):
    rows = pieces[0].shape[1]
    features = w_query.shape[0]
    piece = jax.ShapeDtypeStruct((SIDE, rows, HS), jnp.bfloat16)
    result = pl.pallas_call(
        attend_kernel,
        out_shape=[piece] * 5,
        in_specs=[SMEM] * 4 + [VMEM] * 9,
        out_specs=[VMEM] * 5,
        scratch_shapes=[
            pltpu.VMEM((rows, features), jnp.bfloat16),
            pltpu.VMEM((rows, HS), jnp.bfloat16),
        ],
        cost_estimate=pl.CostEstimate(
            flops=8 * rows * features * HS,
            bytes_accessed=16 * features * HS,
            transcendentals=rows * 1024,
        ),
        name="attend",
    )(table, *lists, *pieces, kv_same, kv_other, gain, w_query, w_out)
    return result[:4], result[4]


def added(first, others):
    total = first.astype(jnp.float32)
    for other in others:
        total = total + other.astype(jnp.float32)
    return total


def on_device(
    patch_tokens,
    obs_tokens,
    footprint,
    list_counts,
    footprint_bias,
    w_query,
    w_key,
    w_value,
    w_out,
    patch_gain,
    obs_gain,
):
    core = lax.axis_index("pipe")
    chip = lax.axis_index("obs")
    place = lax.axis_index("patch")
    patch_count = lax.axis_size("patch")
    chip_row, chip_col = chip // SIDE, chip % SIDE
    near_at = jnp.where(core == 0, chip_col, chip_row)
    far_at = jnp.where(core == 0, chip_row, chip_col)
    near_stride = jnp.where(core == 0, 1, SIDE)
    far_stride = jnp.where(core == 0, SIDE, 1)
    patch_rows = patch_tokens.shape[0] // 2
    obs_rows = obs_tokens.shape[0] // 2
    blocks_here = patch_rows // BLK

    steps = jnp.arange(SIDE)
    back = (far_at - steps)[:, None] % SIDE * far_stride
    ahead = (far_at + steps)[:, None] % SIDE * far_stride
    relative = (near_at - steps)[None, :] % SIDE
    out_table = (ahead + steps[None, :] * near_stride).reshape(-1)
    tail = jnp.stack([place, core, core * blocks_here, 0 * core])
    table_zero = jnp.concatenate(
        [
            (back + relative * near_stride).reshape(-1),
            out_table,
            tail,
            (near_at - steps) % SIDE,
        ]
    ).astype(jnp.int32)
    table_one = jnp.concatenate(
        [(back + steps[None, :] * near_stride).reshape(-1), out_table, tail, steps]
    ).astype(jnp.int32)
    lists = (footprint, list_counts, footprint_bias)

    def by_section(mine):
        theirs = swapped(mine)
        return jnp.where(core == 0, mine, theirs), jnp.where(core == 0, theirs, mine)

    my_obs = lax.dynamic_slice_in_dim(obs_tokens, core * obs_rows, obs_rows, 0)
    my_patch = lax.dynamic_slice_in_dim(patch_tokens, core * patch_rows, patch_rows, 0)
    both = jnp.concatenate([my_obs, my_patch], axis=0)
    group = jnp.stack([both] + [near(both, step) for step in range(1, SIDE)])
    obs_group, patch_group = group[:, :obs_rows], group[:, obs_rows:]
    gains = jnp.concatenate([patch_gain, obs_gain], axis=0).reshape(2, SIDE * SIDE, HS)
    gains = by_section(gains)
    keys_by, values_by = by_section(w_key[0]), by_section(w_value[0])
    query_by, out_by = by_section(w_query[0]), by_section(w_out[0])

    obs_pieces = [obs_group] + [far(obs_group, step) for step in range(1, SIDE)]

    def exchanged(section):
        mine = key_values(
            table_zero, obs_pieces, gains[section][1], keys_by[section], values_by[section]
        )
        gathered = [mine] + [
            lax.ppermute(
                mine, "patch", [(at, (at + step) % patch_count) for at in range(patch_count)]
            )
            for step in range(1, patch_count)
        ]
        same = jnp.stack(gathered)
        return same, swapped(same)

    kv_zero = exchanged(0)
    patch_pieces = [patch_group] + [far(patch_group, step) for step in range(1, SIDE)]
    kv_one = exchanged(1)

    def reduced(parts):
        return added(parts[0], [far(parts[step], step) for step in range(1, SIDE)]).astype(
            jnp.bfloat16
        )

    parts, kept = attend(
        table_zero, lists, patch_pieces, *kv_zero, gains[0][0], query_by[0], out_by[0]
    )
    total = reduced(parts)
    total = added(total, [near(total, step) for step in range(1, SIDE)])
    after_zero = (kept.astype(jnp.float32) + total).astype(jnp.bfloat16)

    pieces = [after_zero] + [far(after_zero, step) for step in range(1, SIDE)]
    parts, _ = attend(table_one, lists, pieces, *kv_one, gains[1][0], query_by[1], out_by[1])
    total = reduced(parts)
    own_zero = lax.dynamic_index_in_dim(after_zero, near_at, 0, keepdims=False)
    own_total = lax.dynamic_index_in_dim(total, near_at, 0, keepdims=False)
    others = [
        near(lax.dynamic_index_in_dim(total, (near_at + step) % SIDE, 0, keepdims=False), step)
        for step in range(1, SIDE)
    ]
    own_one = (own_zero.astype(jnp.float32) + added(own_total, others)).astype(jnp.bfloat16)

    arrived = swapped(jnp.where(core == 0, own_one, own_zero))
    upper = jnp.where(core == 0, own_zero, arrived)
    lower = jnp.where(core == 0, arrived, own_one)
    return jnp.concatenate([upper, lower], axis=0)[None]


def solution(mesh):
    in_specs = (
        P("patch", "obs"),
        P("patch", "obs"),
        P("patch", None),
        P("patch"),
        P("patch", None),
        P("pipe", None, "obs"),
        P("pipe", None, "obs"),
        P("pipe", None, "obs"),
        P("pipe", "obs", None),
        P("pipe", None),
        P("pipe", None),
    )
    out_specs = P("pipe", "patch", "obs")
    return jax.shard_map(
        on_device, mesh=mesh, in_specs=in_specs, out_specs=out_specs, check_vma=False
    )
```

```python
import functools

import jax
import jax.numpy as jnp
from jax import lax
from jax.experimental import pallas as pl
from jax.experimental.pallas import tpu as pltpu
from jax.sharding import PartitionSpec as P


HS = 128
BLK = 128
SIDE = 4
EPS = 1e-05

SMEM = pl.BlockSpec(memory_space=pltpu.SMEM)
VMEM = pl.BlockSpec(memory_space=pltpu.VMEM)
ANY = pl.BlockSpec(memory_space=pl.ANY)
AROUND = (2, 1, 3)


def square_shift(first_axis, step):
    pairs = []
    for core in range(2):
        for row in range(SIDE):
            for col in range(SIDE):
                along_col = (core == 0) == first_axis
                new_row = row if along_col else (row + step) % SIDE
                new_col = (col + step) % SIDE if along_col else col
                base = core * SIDE * SIDE
                pairs.append((base + row * SIDE + col, base + new_row * SIDE + new_col))
    return pairs


def near(value, step):
    return lax.ppermute(value, ("pipe", "obs"), square_shift(True, step))


def far(value, step):
    return lax.ppermute(value, ("pipe", "obs"), square_shift(False, step))


def all_far(value):
    arrived = {step: far(value, step) for step in AROUND}
    return [value] + [arrived[step] for step in range(1, SIDE)]


def all_near(value):
    arrived = {step: near(value, step) for step in AROUND}
    return [value] + [arrived[step] for step in range(1, SIDE)]


def swapped(value):
    return lax.ppermute(value, "pipe", [(0, 1), (1, 0)])


def position():
    core = lax.axis_index("pipe")
    chip = lax.axis_index("obs")
    row = lax.div(chip, SIDE)
    col = lax.rem(chip, SIDE)
    near_at = jnp.where(core == 0, col, row)
    far_at = jnp.where(core == 0, row, col)
    near_stride = jnp.where(core == 0, 1, SIDE)
    far_stride = jnp.where(core == 0, SIDE, 1)
    return core, near_at, far_at, near_stride, far_stride


def wrapped(value):
    return lax.rem(value + SIDE, SIDE)


def tile_cols(block):
    return pl.ds(pl.multiple_of(block * HS, HS), HS)


def fetch(core, section, mine, theirs, target, sem, act):
    @pl.when(core == section)
    def _():
        act(pltpu.make_async_copy(mine, target, sem))

    @pl.when(core != section)
    def _():
        act(pltpu.make_async_copy(theirs, target, sem))


def start(copy):
    copy.start()


def wait(copy):
    copy.wait()


def normed_into(where, is_relative, pieces, gain, normed):
    _, near_at, far_at, near_stride, far_stride = where
    rows = normed.shape[0]
    squares = jnp.zeros((rows, HS), jnp.float32)
    for piece in pieces:
        for part in range(SIDE):
            widened = piece[part].astype(jnp.float32)
            squares = squares + widened * widened
    mean = jnp.sum(squares, axis=-1, keepdims=True) * (1.0 / (SIDE * SIDE * HS))
    inverse = lax.rsqrt(mean + EPS)
    for step, piece in enumerate(pieces):
        for part in range(SIDE):
            at = wrapped(near_at - part) if is_relative else part
            block = wrapped(far_at - step) * far_stride + at * near_stride
            scaled = (piece[part].astype(jnp.float32) * inverse) * gain[pl.ds(block, 1), :]
            normed[:, tile_cols(block)] = scaled.astype(jnp.bfloat16)


def chosen_gain(core, section, mine, theirs, index, gain):
    gain[...] = jnp.where(core == section, mine[index], theirs[index])


def key_value_kernel(
    section,
    o0,
    o1,
    o2,
    o3,
    gain_mine,
    gain_theirs,
    key_mine,
    key_theirs,
    value_mine,
    value_theirs,
    out,
    normed,
    weight,
    gain,
    sems,
):
    where = position()
    core = where[0]
    key_at, value_at = weight.at[:, :HS], weight.at[:, HS:]
    fetch(core, section, key_mine, key_theirs, key_at, sems.at[0], start)
    fetch(core, section, value_mine, value_theirs, value_at, sems.at[1], start)
    chosen_gain(core, section, gain_mine, gain_theirs, 1, gain)
    normed_into(where, True, (o0, o1, o2, o3), gain, normed)
    fetch(core, section, key_mine, key_theirs, key_at, sems.at[0], wait)
    fetch(core, section, value_mine, value_theirs, value_at, sems.at[1], wait)
    out[...] = jnp.dot(
        normed[...], weight[...], preferred_element_type=jnp.float32
    ).astype(jnp.bfloat16)


def attend_kernel(
    section,
    entries,
    counts,
    bias,
    x0,
    x1,
    x2,
    x3,
    kv_same,
    kv_other,
    gain_mine,
    gain_theirs,
    query_mine,
    query_theirs,
    out_mine,
    out_theirs,
    y0,
    y1,
    y2,
    y3,
    kept,
    normed,
    context,
    w_query,
    w_out,
    gain,
    sems,
):
    rows = normed.shape[0]
    slots = entries.shape[1]
    where = position()
    core, near_at, far_at, near_stride, far_stride = where
    place = lax.axis_index("patch")
    patch_count = kv_same.shape[0]
    fetch(core, section, query_mine, query_theirs, w_query, sems.at[0], start)
    fetch(core, section, out_mine, out_theirs, w_out, sems.at[1], start)
    chosen_gain(core, section, gain_mine, gain_theirs, 0, gain)
    normed_into(where, section == 0, (x0, x1, x2, x3), gain, normed)
    if section == 0:
        for part in range(SIDE):
            kept[part] = x0[wrapped(near_at - part)]
    fetch(core, section, query_mine, query_theirs, w_query, sems.at[0], wait)
    queries = (
        jnp.dot(normed[...], w_query[...], preferred_element_type=jnp.float32) * HS ** (-0.5)
    ).astype(jnp.bfloat16)
    blocks_here = rows // BLK
    for block in range(blocks_here):
        query = queries[block * BLK : (block + 1) * BLK]
        row = core * blocks_here + block
        live = counts[row]
        scores, values = [], []
        for slot in range(slots):
            entry = jnp.where(slot < live, entries[row, slot], 0)
            owner = lax.div(entry, 2)
            index = owner
            if section == 0:
                index = lax.rem(place - owner + patch_count, patch_count)
            is_same = (entry - owner * 2) == core
            both = jnp.where(is_same, kv_same[index], kv_other[index])
            score = lax.dot_general(
                query,
                both[:, :HS],
                (((1,), (1,)), ((), ())),
                preferred_element_type=jnp.float32,
            )
            scores.append(jnp.where(slot < live, score + bias[row, slot], -1e30))
            values.append(both[:, HS:])
        scores = jnp.concatenate(scores, axis=1)
        top = jnp.max(scores, axis=-1, keepdims=True)
        weights = jnp.exp(scores - top)
        weights = (weights / jnp.sum(weights, axis=-1, keepdims=True)).astype(jnp.bfloat16)
        context[block * BLK : (block + 1) * BLK, :] = jnp.dot(
            weights, jnp.concatenate(values, axis=0), preferred_element_type=jnp.float32
        ).astype(jnp.bfloat16)
    fetch(core, section, out_mine, out_theirs, w_out, sems.at[1], wait)
    ready = context[...]
    width = SIDE * HS
    for part in range(SIDE):
        normed[:, part * width : (part + 1) * width] = jnp.dot(
            ready, w_out[:, part * width : (part + 1) * width], preferred_element_type=jnp.float32
        ).astype(jnp.bfloat16)
    for step, out in enumerate((y0, y1, y2, y3)):
        for part in range(SIDE):
            block = wrapped(far_at + step) * far_stride + part * near_stride
            out[part] = normed[:, tile_cols(block)]


def key_values(section, pieces, gains, w_key, w_value):
    rows = pieces[0].shape[1]
    features = w_key[0].shape[0]
    return pl.pallas_call(
        functools.partial(key_value_kernel, section),
        out_shape=jax.ShapeDtypeStruct((rows, 2 * HS), jnp.bfloat16),
        in_specs=[VMEM] * 6 + [ANY] * 4,
        out_specs=VMEM,
        scratch_shapes=[
            pltpu.VMEM((rows, features), jnp.bfloat16),
            pltpu.VMEM((features, 2 * HS), jnp.bfloat16),
            pltpu.VMEM(gains[0].shape[1:], jnp.float32),
            pltpu.SemaphoreType.DMA((2,)),
        ],
        cost_estimate=pl.CostEstimate(
            flops=4 * rows * features * HS, bytes_accessed=6 * features * HS, transcendentals=0
        ),
        compiler_params=pltpu.CompilerParams(vmem_limit_bytes=8 << 20),
        name="key_values",
    )(*pieces, *gains, *w_key, *w_value)


def attend(section, lists, pieces, kv, gains, w_query, w_out):
    rows = pieces[0].shape[1]
    features = w_query[0].shape[0]
    piece = jax.ShapeDtypeStruct((SIDE, rows, HS), jnp.bfloat16)
    extra = piece if section == 0 else jax.ShapeDtypeStruct((8, HS), jnp.bfloat16)
    return pl.pallas_call(
        functools.partial(attend_kernel, section),
        out_shape=[piece] * SIDE + [extra],
        in_specs=[SMEM] * 3 + [VMEM] * 8 + [ANY] * 4,
        out_specs=[VMEM] * 5,
        scratch_shapes=[
            pltpu.VMEM((rows, features), jnp.bfloat16),
            pltpu.VMEM((rows, HS), jnp.bfloat16),
            pltpu.VMEM(w_query[0].shape, jnp.bfloat16),
            pltpu.VMEM(w_out[0].shape, jnp.bfloat16),
            pltpu.VMEM(gains[0].shape[1:], jnp.float32),
            pltpu.SemaphoreType.DMA((2,)),
        ],
        cost_estimate=pl.CostEstimate(
            flops=8 * rows * features * HS,
            bytes_accessed=16 * features * HS,
            transcendentals=rows * 1024,
        ),
        compiler_params=pltpu.CompilerParams(vmem_limit_bytes=12 << 20),
        name="attend",
    )(*lists, *pieces, *kv, *gains, *w_query, *w_out)


def added(first, others):
    total = first.astype(jnp.float32)
    for other in others:
        total = total + other.astype(jnp.float32)
    return total


def on_device(
    patch_tokens,
    obs_tokens,
    footprint,
    list_counts,
    footprint_bias,
    w_query,
    w_key,
    w_value,
    w_out,
    patch_gain,
    obs_gain,
):
    core, near_at, _, _, _ = position()
    patch_count = lax.axis_size("patch")
    patch_rows = patch_tokens.shape[0] // 2
    obs_rows = obs_tokens.shape[0] // 2
    lists = (footprint, list_counts, footprint_bias)

    my_obs = lax.dynamic_slice_in_dim(obs_tokens, core * obs_rows, obs_rows, 0)
    my_patch = lax.dynamic_slice_in_dim(patch_tokens, core * patch_rows, patch_rows, 0)
    group = jnp.stack(all_near(jnp.concatenate([my_obs, my_patch], axis=0)))
    obs_group, patch_group = group[:, :obs_rows], group[:, obs_rows:]

    gains = jnp.concatenate([patch_gain, obs_gain], axis=0).reshape(2, SIDE * SIDE, HS)
    gains, keys, values, queries, outs = [
        (mine, swapped(mine)) for mine in (gains, w_key[0], w_value[0], w_query[0], w_out[0])
    ]

    obs_pieces = all_far(obs_group)
    mine = key_values(0, obs_pieces, gains, keys, values)
    steps = sorted(range(1, patch_count), key=lambda step: -min(step, patch_count - step))
    arrived = {}
    for step in steps:
        pairs = [(at, (at + step) % patch_count) for at in range(patch_count)]
        arrived[step] = lax.ppermute(mine, "patch", pairs)
    same = jnp.stack([mine] + [arrived[step] for step in range(1, patch_count)])
    kv_zero = (same, swapped(same))
    patch_group, mine = lax.optimization_barrier((patch_group, mine))
    patch_pieces = all_far(patch_group)
    mine = key_values(1, obs_pieces, gains, keys, values)

    def reduced(parts):
        arrived = {step: far(parts[step], step) for step in AROUND}
        return added(parts[0], [arrived[step] for step in range(1, SIDE)]).astype(jnp.bfloat16)

    *parts, kept = attend(0, lists, patch_pieces, kv_zero, gains, queries, outs)
    mine, _ = lax.optimization_barrier((mine, kept))
    same = lax.all_to_all(jnp.broadcast_to(mine[None], (patch_count, *mine.shape)), "patch", 0, 0)
    kv_one = (same, swapped(same))

    total = reduced(parts)
    first, *others = all_near(total)
    after_zero = (kept.astype(jnp.float32) + added(first, others)).astype(jnp.bfloat16)

    *parts, _ = attend(1, lists, all_far(after_zero), kv_one, gains, queries, outs)
    total = reduced(parts)
    own_zero = lax.dynamic_index_in_dim(after_zero, near_at, 0, keepdims=False)
    own_total = lax.dynamic_index_in_dim(total, near_at, 0, keepdims=False)
    others = [
        near(lax.dynamic_index_in_dim(total, wrapped(near_at + step), 0, keepdims=False), step)
        for step in AROUND
    ]
    own_one = (own_zero.astype(jnp.float32) + added(own_total, others)).astype(jnp.bfloat16)

    arrived = swapped(jnp.where(core == 0, own_one, own_zero))
    upper = jnp.where(core == 0, own_zero, arrived)
    lower = jnp.where(core == 0, arrived, own_one)
    return jnp.concatenate([upper, lower], axis=0)[None]


def solution(mesh):
    in_specs = (
        P("patch", "obs"),
        P("patch", "obs"),
        P("patch", None),
        P("patch"),
        P("patch", None),
        P("pipe", None, "obs"),
        P("pipe", None, "obs"),
        P("pipe", None, "obs"),
        P("pipe", "obs", None),
        P("pipe", None),
        P("pipe", None),
    )
    out_specs = P("pipe", "patch", "obs")
    return jax.shard_map(
        on_device, mesh=mesh, in_specs=in_specs, out_specs=out_specs, check_vma=False
    )
```

```python
import functools

import jax
import jax.numpy as jnp
from jax import lax
from jax.experimental import pallas as pl
from jax.experimental.pallas import tpu as pltpu
from jax.sharding import PartitionSpec as P


HS = 128
BLK = 128
SIDE = 4
EPS = 1e-05

SMEM = pl.BlockSpec(memory_space=pltpu.SMEM)
VMEM = pl.BlockSpec(memory_space=pltpu.VMEM)
ANY = pl.BlockSpec(memory_space=pl.ANY)
AROUND = (2, 1, 3)


def square_shift(first_axis, step):
    pairs = []
    for core in range(2):
        for row in range(SIDE):
            for col in range(SIDE):
                along_col = (core == 0) == first_axis
                new_row = row if along_col else (row + step) % SIDE
                new_col = (col + step) % SIDE if along_col else col
                base = core * SIDE * SIDE
                pairs.append((base + row * SIDE + col, base + new_row * SIDE + new_col))
    return pairs


def near(value, step):
    return lax.ppermute(value, ("pipe", "obs"), square_shift(True, step))


def far(value, step):
    return lax.ppermute(value, ("pipe", "obs"), square_shift(False, step))


def all_far(value):
    arrived = {step: far(value, step) for step in AROUND}
    return [value] + [arrived[step] for step in range(1, SIDE)]


def all_near(value):
    arrived = {step: near(value, step) for step in AROUND}
    return [value] + [arrived[step] for step in range(1, SIDE)]


def swapped(value):
    return lax.ppermute(value, "pipe", [(0, 1), (1, 0)])


def position():
    core = lax.axis_index("pipe")
    chip = lax.axis_index("obs")
    row = lax.div(chip, SIDE)
    col = lax.rem(chip, SIDE)
    near_at = jnp.where(core == 0, col, row)
    far_at = jnp.where(core == 0, row, col)
    near_stride = jnp.where(core == 0, 1, SIDE)
    far_stride = jnp.where(core == 0, SIDE, 1)
    return core, near_at, far_at, near_stride, far_stride


def wrapped(value):
    return lax.rem(value + SIDE, SIDE)


def tile_cols(block):
    return pl.ds(pl.multiple_of(block * HS, HS), HS)


def for_core(core, copies, act):
    for number in range(2):

        @pl.when(core == number)
        def _(number=number):
            for copy in copies(number):
                act(copy)


def start(copy):
    copy.start()


def wait(copy):
    copy.wait()


def placed(where, is_relative):
    _, near_at, far_at, near_stride, far_stride = where

    def block(step, part):
        at = wrapped(near_at - part) if is_relative else part
        return wrapped(far_at - step) * far_stride + at * near_stride

    return block


def normed_into(block_of, pieces, gain, normed):
    rows = normed.shape[0]
    squares = jnp.zeros((rows, HS), jnp.float32)
    for piece in pieces:
        for part in range(SIDE):
            widened = piece[part].astype(jnp.float32)
            squares = squares + widened * widened
    mean = jnp.sum(squares, axis=-1, keepdims=True) * (1.0 / (SIDE * SIDE * HS))
    inverse = lax.rsqrt(mean + EPS)
    for step, piece in enumerate(pieces):
        for part in range(SIDE):
            block = block_of(step, part)
            scaled = (piece[part].astype(jnp.float32) * inverse) * gain[pl.ds(block, 1), :]
            normed[:, tile_cols(block)] = scaled.astype(jnp.bfloat16)


def chosen_gain(core, section, mine, theirs, index, gain):
    gain[...] = jnp.where(core == section, mine[index], theirs[index])


def key_value_kernel(
    section,
    o0,
    o1,
    o2,
    o3,
    gain_mine,
    gain_theirs,
    key_mine,
    key_theirs,
    value_mine,
    value_theirs,
    keep,
    give,
    normed,
    weight,
    gain,
    sems,
):
    where = position()
    core = where[0]

    def copies(number):
        key = key_mine if number == section else key_theirs
        value = value_mine if number == section else value_theirs
        halves = (weight.at[:, :HS], weight.at[:, HS:])
        yield pltpu.make_async_copy(key, halves[number], sems.at[0])
        yield pltpu.make_async_copy(value, halves[1 - number], sems.at[1])

    for_core(core, copies, start)
    chosen_gain(core, section, gain_mine, gain_theirs, 1, gain)
    normed_into(placed(where, True), (o0, o1, o2, o3), gain, normed)
    for_core(core, copies, wait)
    both = jnp.dot(normed[...], weight[...], preferred_element_type=jnp.float32)
    keep[...] = both[:, :HS].astype(jnp.bfloat16)
    give[...] = both[:, HS:].astype(jnp.bfloat16)


def attend_kernel(
    section,
    entries,
    counts,
    bias,
    x0,
    x1,
    x2,
    x3,
    kv_mine,
    kv_theirs,
    gain_mine,
    gain_theirs,
    query_mine,
    query_theirs,
    out_mine,
    out_theirs,
    y0,
    y1,
    y2,
    y3,
    kept,
    normed,
    context,
    w_query,
    w_out,
    gain,
    sems,
):
    rows = normed.shape[0]
    slots = entries.shape[1]
    where = position()
    core, near_at, far_at, near_stride, far_stride = where

    def query_copy(number):
        yield pltpu.make_async_copy(
            query_mine if number == section else query_theirs, w_query, sems.at[0]
        )

    def out_copy(number):
        yield pltpu.make_async_copy(
            out_mine if number == section else out_theirs, w_out, sems.at[1]
        )

    for_core(core, query_copy, start)
    for_core(core, out_copy, start)
    chosen_gain(core, section, gain_mine, gain_theirs, 0, gain)
    normed_into(placed(where, section == 0), (x0, x1, x2, x3), gain, normed)
    if section == 0:
        for part in range(SIDE):
            kept[part] = x0[wrapped(near_at - part)]
    for_core(core, query_copy, wait)
    queries = (
        jnp.dot(normed[...], w_query[...], preferred_element_type=jnp.float32) * HS ** (-0.5)
    ).astype(jnp.bfloat16)
    blocks_here = rows // BLK
    for block in range(blocks_here):
        query = queries[block * BLK : (block + 1) * BLK]
        row = core * blocks_here + block
        live = counts[row]
        scores, values = [], []
        for slot in range(slots):
            owner = jnp.where(slot < live, lax.div(entries[row, slot], 2), 0)
            mine, theirs = kv_mine[owner], kv_theirs[owner]
            score = lax.dot_general(
                query,
                jnp.where(core == 0, mine, theirs),
                (((1,), (1,)), ((), ())),
                preferred_element_type=jnp.float32,
            )
            scores.append(jnp.where(slot < live, score + bias[row, slot], -1e30))
            values.append(jnp.where(core == 0, theirs, mine))
        scores = jnp.concatenate(scores, axis=1)
        top = jnp.max(scores, axis=-1, keepdims=True)
        weights = jnp.exp(scores - top)
        weights = (weights / jnp.sum(weights, axis=-1, keepdims=True)).astype(jnp.bfloat16)
        context[block * BLK : (block + 1) * BLK, :] = jnp.dot(
            weights, jnp.concatenate(values, axis=0), preferred_element_type=jnp.float32
        ).astype(jnp.bfloat16)
    for_core(core, out_copy, wait)
    ready = context[...]
    width = SIDE * HS
    for part in range(SIDE):
        normed[:, part * width : (part + 1) * width] = jnp.dot(
            ready, w_out[:, part * width : (part + 1) * width], preferred_element_type=jnp.float32
        ).astype(jnp.bfloat16)
    for step, out in enumerate((y0, y1, y2, y3)):
        for part in range(SIDE):
            block = wrapped(far_at + step) * far_stride + part * near_stride
            out[part] = normed[:, tile_cols(block)]


def key_values(section, pieces, gains, w_key, w_value):
    rows = pieces[0].shape[1]
    features = w_key[0].shape[0]
    return pl.pallas_call(
        functools.partial(key_value_kernel, section),
        out_shape=[jax.ShapeDtypeStruct((rows, HS), jnp.bfloat16)] * 2,
        in_specs=[VMEM] * 6 + [ANY] * 4,
        out_specs=[VMEM] * 2,
        scratch_shapes=[
            pltpu.VMEM((rows, features), jnp.bfloat16),
            pltpu.VMEM((features, 2 * HS), jnp.bfloat16),
            pltpu.VMEM(gains[0].shape[1:], jnp.float32),
            pltpu.SemaphoreType.DMA((2,)),
        ],
        cost_estimate=pl.CostEstimate(
            flops=4 * rows * features * HS, bytes_accessed=6 * features * HS, transcendentals=0
        ),
        compiler_params=pltpu.CompilerParams(vmem_limit_bytes=8 << 20),
        name="key_values",
    )(*pieces, *gains, *w_key, *w_value)


def attend(section, lists, pieces, kv, gains, w_query, w_out):
    rows = pieces[0].shape[1]
    features = w_query[0].shape[0]
    piece = jax.ShapeDtypeStruct((SIDE, rows, HS), jnp.bfloat16)
    extra = piece if section == 0 else jax.ShapeDtypeStruct((8, HS), jnp.bfloat16)
    return pl.pallas_call(
        functools.partial(attend_kernel, section),
        out_shape=[piece] * SIDE + [extra],
        in_specs=[SMEM] * 3 + [VMEM] * 8 + [ANY] * 4,
        out_specs=[VMEM] * 5,
        scratch_shapes=[
            pltpu.VMEM((rows, features), jnp.bfloat16),
            pltpu.VMEM((rows, HS), jnp.bfloat16),
            pltpu.VMEM(w_query[0].shape, jnp.bfloat16),
            pltpu.VMEM(w_out[0].shape, jnp.bfloat16),
            pltpu.VMEM(gains[0].shape[1:], jnp.float32),
            pltpu.SemaphoreType.DMA((2,)),
        ],
        cost_estimate=pl.CostEstimate(
            flops=8 * rows * features * HS,
            bytes_accessed=16 * features * HS,
            transcendentals=rows * 1024,
        ),
        compiler_params=pltpu.CompilerParams(vmem_limit_bytes=12 << 20),
        name="attend",
    )(*lists, *pieces, *kv, *gains, *w_query, *w_out)


def added(first, others):
    total = first.astype(jnp.float32)
    for other in others:
        total = total + other.astype(jnp.float32)
    return total


def on_device(
    patch_tokens,
    obs_tokens,
    footprint,
    list_counts,
    footprint_bias,
    w_query,
    w_key,
    w_value,
    w_out,
    patch_gain,
    obs_gain,
):
    core, near_at, _, _, _ = position()
    patch_count = lax.axis_size("patch")
    patch_rows = patch_tokens.shape[0] // 2
    obs_rows = obs_tokens.shape[0] // 2
    lists = (footprint, list_counts, footprint_bias)

    my_obs = lax.dynamic_slice_in_dim(obs_tokens, core * obs_rows, obs_rows, 0)
    my_patch = lax.dynamic_slice_in_dim(patch_tokens, core * patch_rows, patch_rows, 0)
    group = jnp.stack(all_near(jnp.concatenate([my_obs, my_patch], axis=0)))
    obs_group, patch_group = group[:, :obs_rows], group[:, obs_rows:]
    obs_pieces = all_far(obs_group)

    live = jnp.arange(footprint.shape[1])[None, :] < list_counts[:, None]
    owners = jnp.arange(patch_count)[:, None, None]
    named = live[None] & (footprint[None] // 2 == owners)
    needed = jnp.max(jnp.where(named, footprint[None] % 2, 0), axis=(1, 2)).astype(jnp.int32)
    needs = lax.all_to_all(
        jnp.broadcast_to(needed[:, None, None], (patch_count, 8, HS)), "patch", 0, 0
    )[:, :1]

    gains = jnp.concatenate([patch_gain, obs_gain], axis=0).reshape(2, SIDE * SIDE, HS)
    gains, keys, values, queries, outs = [
        (mine, swapped(mine)) for mine in (gains, w_key[0], w_value[0], w_query[0], w_out[0])
    ]

    def chosen(section):
        keep, give = key_values(section, obs_pieces, gains, keys, values)
        return keep, swapped(give), needs

    def exchanged(keep, given, needs):
        pieces = jnp.where(needs == core, keep[None], given[None])
        mine = lax.all_to_all(pieces, "patch", 0, 0)
        return mine, swapped(mine)

    kv_zero = exchanged(*chosen(0))
    patch_pieces = all_far(patch_group)
    pieces_one = chosen(1)

    def reduced(parts):
        arrived = {step: far(parts[step], step) for step in AROUND}
        return added(parts[0], [arrived[step] for step in range(1, SIDE)]).astype(jnp.bfloat16)

    *parts, kept = attend(0, lists, patch_pieces, kv_zero, gains, queries, outs)
    pieces_one, _ = lax.optimization_barrier((pieces_one, kept))
    kv_one = exchanged(*pieces_one)

    total = reduced(parts)
    first, *others = all_near(total)
    after_zero = (kept.astype(jnp.float32) + added(first, others)).astype(jnp.bfloat16)

    pieces = all_far(after_zero)
    *parts, _ = attend(1, lists, pieces, kv_one, gains, queries, outs)
    total = reduced(parts)
    own_zero = lax.dynamic_index_in_dim(after_zero, near_at, 0, keepdims=False)
    own_total = lax.dynamic_index_in_dim(total, near_at, 0, keepdims=False)
    others = [
        near(lax.dynamic_index_in_dim(total, wrapped(near_at + step), 0, keepdims=False), step)
        for step in AROUND
    ]
    own_one = (own_zero.astype(jnp.float32) + added(own_total, others)).astype(jnp.bfloat16)

    arrived = swapped(jnp.where(core == 0, own_one, own_zero))
    upper = jnp.where(core == 0, own_zero, arrived)
    lower = jnp.where(core == 0, arrived, own_one)
    return jnp.concatenate([upper, lower], axis=0)[None]


def solution(mesh):
    in_specs = (
        P("patch", "obs"),
        P("patch", "obs"),
        P("patch", None),
        P("patch"),
        P("patch", None),
        P("pipe", None, "obs"),
        P("pipe", None, "obs"),
        P("pipe", None, "obs"),
        P("pipe", "obs", None),
        P("pipe", None),
        P("pipe", None),
    )
    out_specs = P("pipe", "patch", "obs")
    return jax.shard_map(
        on_device, mesh=mesh, in_specs=in_specs, out_specs=out_specs, check_vma=False
    )
```

```python
import functools

import jax
import jax.numpy as jnp
from jax import lax
from jax.experimental import pallas as pl
from jax.experimental.pallas import tpu as pltpu
from jax.sharding import PartitionSpec as P


HS = 128
BLK = 128
SIDE = 4
EPS = 1e-05

SMEM = pl.BlockSpec(memory_space=pltpu.SMEM)
VMEM = pl.BlockSpec(memory_space=pltpu.VMEM)
ANY = pl.BlockSpec(memory_space=pl.ANY)
AROUND = (2, 1, 3)


def square_shift(first_axis, step):
    pairs = []
    for core in range(2):
        for row in range(SIDE):
            for col in range(SIDE):
                along_col = (core == 0) == first_axis
                new_row = row if along_col else (row + step) % SIDE
                new_col = (col + step) % SIDE if along_col else col
                base = core * SIDE * SIDE
                pairs.append((base + row * SIDE + col, base + new_row * SIDE + new_col))
    return pairs


def near(value, step):
    return lax.ppermute(value, ("pipe", "obs"), square_shift(True, step))


def far(value, step):
    return lax.ppermute(value, ("pipe", "obs"), square_shift(False, step))


def all_far(value):
    arrived = {step: far(value, step) for step in AROUND}
    return [value] + [arrived[step] for step in range(1, SIDE)]


def all_near(value):
    arrived = {step: near(value, step) for step in AROUND}
    return [value] + [arrived[step] for step in range(1, SIDE)]


def swapped(value):
    return lax.ppermute(value, "pipe", [(0, 1), (1, 0)])


def position():
    core = lax.axis_index("pipe")
    chip = lax.axis_index("obs")
    row = lax.div(chip, SIDE)
    col = lax.rem(chip, SIDE)
    near_at = jnp.where(core == 0, col, row)
    far_at = jnp.where(core == 0, row, col)
    near_stride = jnp.where(core == 0, 1, SIDE)
    far_stride = jnp.where(core == 0, SIDE, 1)
    return core, near_at, far_at, near_stride, far_stride


def wrapped(value):
    return lax.rem(value + SIDE, SIDE)


def tile_cols(block):
    return pl.ds(pl.multiple_of(block * HS, HS), HS)


def fetch(core, section, mine, theirs, target, sem, act):
    @pl.when(core == section)
    def _():
        act(pltpu.make_async_copy(mine, target, sem))

    @pl.when(core != section)
    def _():
        act(pltpu.make_async_copy(theirs, target, sem))


def start(copy):
    copy.start()


def wait(copy):
    copy.wait()


def natural(step, part):
    return step * SIDE + part


def placed(where, is_relative):
    _, near_at, far_at, near_stride, far_stride = where

    def block(step, part):
        at = wrapped(near_at - part) if is_relative else part
        return wrapped(far_at - step) * far_stride + at * near_stride

    return block


def normed_into(block_of, pieces, gain, normed):
    rows = normed.shape[0]
    squares = jnp.zeros((rows, HS), jnp.float32)
    for piece in pieces:
        for part in range(SIDE):
            widened = piece[part].astype(jnp.float32)
            squares = squares + widened * widened
    mean = jnp.sum(squares, axis=-1, keepdims=True) * (1.0 / (SIDE * SIDE * HS))
    inverse = lax.rsqrt(mean + EPS)
    for step, piece in enumerate(pieces):
        for part in range(SIDE):
            block = block_of(step, part)
            scaled = (piece[part].astype(jnp.float32) * inverse) * gain[pl.ds(block, 1), :]
            normed[:, tile_cols(block)] = scaled.astype(jnp.bfloat16)


def chosen_gain(core, section, mine, theirs, index, gain):
    gain[...] = jnp.where(core == section, mine[index], theirs[index])


def key_value_kernel(
    section,
    obs,
    gain_mine,
    gain_theirs,
    key_mine,
    key_theirs,
    value_mine,
    value_theirs,
    out,
    normed,
    weight,
    gain,
    sems,
):
    core = lax.axis_index("pipe")
    key_at, value_at = weight.at[:, :HS], weight.at[:, HS:]
    fetch(core, section, key_mine, key_theirs, key_at, sems.at[0], start)
    fetch(core, section, value_mine, value_theirs, value_at, sems.at[1], start)
    chosen_gain(core, section, gain_mine, gain_theirs, 1, gain)
    pieces = [obs.at[step * SIDE : (step + 1) * SIDE] for step in range(SIDE)]
    normed_into(natural, pieces, gain, normed)
    fetch(core, section, key_mine, key_theirs, key_at, sems.at[0], wait)
    fetch(core, section, value_mine, value_theirs, value_at, sems.at[1], wait)
    out[...] = jnp.dot(
        normed[...], weight[...], preferred_element_type=jnp.float32
    ).astype(jnp.bfloat16)


def attend_kernel(
    section,
    entries,
    counts,
    bias,
    x0,
    x1,
    x2,
    x3,
    kv_same,
    kv_other,
    gain_mine,
    gain_theirs,
    query_mine,
    query_theirs,
    out_mine,
    out_theirs,
    y0,
    y1,
    y2,
    y3,
    kept,
    normed,
    context,
    w_query,
    w_out,
    gain,
    sems,
):
    rows = normed.shape[0]
    slots = entries.shape[1]
    where = position()
    core, near_at, far_at, near_stride, far_stride = where
    place = lax.axis_index("patch")
    patch_count = kv_same.shape[0]
    fetch(core, section, query_mine, query_theirs, w_query, sems.at[0], start)
    fetch(core, section, out_mine, out_theirs, w_out, sems.at[1], start)
    chosen_gain(core, section, gain_mine, gain_theirs, 0, gain)
    normed_into(placed(where, section == 0), (x0, x1, x2, x3), gain, normed)
    if section == 0:
        for part in range(SIDE):
            kept[part] = x0[wrapped(near_at - part)]
    fetch(core, section, query_mine, query_theirs, w_query, sems.at[0], wait)
    queries = (
        jnp.dot(normed[...], w_query[...], preferred_element_type=jnp.float32) * HS ** (-0.5)
    ).astype(jnp.bfloat16)
    blocks_here = rows // BLK
    for block in range(blocks_here):
        query = queries[block * BLK : (block + 1) * BLK]
        row = core * blocks_here + block
        live = counts[row]
        scores, values = [], []
        for slot in range(slots):
            entry = jnp.where(slot < live, entries[row, slot], 0)
            owner = lax.div(entry, 2)
            index = lax.rem(place - owner + patch_count, patch_count)
            is_same = (entry - owner * 2) == core
            both = jnp.where(is_same, kv_same[index], kv_other[index])
            score = lax.dot_general(
                query,
                both[:, :HS],
                (((1,), (1,)), ((), ())),
                preferred_element_type=jnp.float32,
            )
            scores.append(jnp.where(slot < live, score + bias[row, slot], -1e30))
            values.append(both[:, HS:])
        scores = jnp.concatenate(scores, axis=1)
        top = jnp.max(scores, axis=-1, keepdims=True)
        weights = jnp.exp(scores - top)
        weights = (weights * (1.0 / jnp.sum(weights, axis=-1, keepdims=True))).astype(jnp.bfloat16)
        context[block * BLK : (block + 1) * BLK, :] = jnp.dot(
            weights, jnp.concatenate(values, axis=0), preferred_element_type=jnp.float32
        ).astype(jnp.bfloat16)
    fetch(core, section, out_mine, out_theirs, w_out, sems.at[1], wait)
    ready = context[...]
    width = SIDE * HS
    for part in range(SIDE):
        normed[:, part * width : (part + 1) * width] = jnp.dot(
            ready, w_out[:, part * width : (part + 1) * width], preferred_element_type=jnp.float32
        ).astype(jnp.bfloat16)
    for step, out in enumerate((y0, y1, y2, y3)):
        for part in range(SIDE):
            block = wrapped(far_at + step) * far_stride + part * near_stride
            out[part] = normed[:, tile_cols(block)]


def key_values(section, obs, gains, w_key, w_value):
    rows = obs.shape[1]
    features = w_key[0].shape[0]
    return pl.pallas_call(
        functools.partial(key_value_kernel, section),
        out_shape=jax.ShapeDtypeStruct((rows, 2 * HS), jnp.bfloat16),
        in_specs=[VMEM] * 3 + [ANY] * 4,
        out_specs=VMEM,
        scratch_shapes=[
            pltpu.VMEM((rows, features), jnp.bfloat16),
            pltpu.VMEM((features, 2 * HS), jnp.bfloat16),
            pltpu.VMEM(gains[0].shape[1:], jnp.float32),
            pltpu.SemaphoreType.DMA((2,)),
        ],
        cost_estimate=pl.CostEstimate(
            flops=4 * rows * features * HS, bytes_accessed=6 * features * HS, transcendentals=0
        ),
        compiler_params=pltpu.CompilerParams(vmem_limit_bytes=8 << 20),
        name="key_values",
    )(obs, *gains, *w_key, *w_value)


def attend(section, lists, pieces, kv, gains, w_query, w_out):
    rows = pieces[0].shape[1]
    features = w_query[0].shape[0]
    piece = jax.ShapeDtypeStruct((SIDE, rows, HS), jnp.bfloat16)
    extra = piece if section == 0 else jax.ShapeDtypeStruct((8, HS), jnp.bfloat16)
    return pl.pallas_call(
        functools.partial(attend_kernel, section),
        out_shape=[piece] * SIDE + [extra],
        in_specs=[SMEM] * 3 + [VMEM] * 8 + [ANY] * 4,
        out_specs=[VMEM] * 5,
        scratch_shapes=[
            pltpu.VMEM((rows, features), jnp.bfloat16),
            pltpu.VMEM((rows, HS), jnp.bfloat16),
            pltpu.VMEM(w_query[0].shape, jnp.bfloat16),
            pltpu.VMEM(w_out[0].shape, jnp.bfloat16),
            pltpu.VMEM(gains[0].shape[1:], jnp.float32),
            pltpu.SemaphoreType.DMA((2,)),
        ],
        cost_estimate=pl.CostEstimate(
            flops=8 * rows * features * HS,
            bytes_accessed=16 * features * HS,
            transcendentals=rows * 1024,
        ),
        compiler_params=pltpu.CompilerParams(vmem_limit_bytes=12 << 20),
        name="attend",
    )(*lists, *pieces, *kv, *gains, *w_query, *w_out)


def added(first, others):
    total = first.astype(jnp.float32)
    for other in others:
        total = total + other.astype(jnp.float32)
    return total


def on_device(
    patch_tokens,
    obs_tokens,
    footprint,
    list_counts,
    footprint_bias,
    w_query,
    w_key,
    w_value,
    w_out,
    patch_gain,
    obs_gain,
):
    core, near_at, _, _, _ = position()
    patch_count = lax.axis_size("patch")
    patch_rows = patch_tokens.shape[0] // 2
    obs_rows = obs_tokens.shape[0] // 2
    lists = (footprint, list_counts, footprint_bias)

    my_obs = lax.dynamic_slice_in_dim(obs_tokens, core * obs_rows, obs_rows, 0)
    obs = lax.all_to_all(
        jnp.broadcast_to(my_obs[None], (lax.axis_size("obs"), *my_obs.shape)), "obs", 0, 0
    )
    my_patch = lax.dynamic_slice_in_dim(patch_tokens, core * patch_rows, patch_rows, 0)
    patch_group = jnp.stack(all_near(my_patch))

    gains = jnp.concatenate([patch_gain, obs_gain], axis=0).reshape(2, SIDE * SIDE, HS)
    gains, keys, values, queries, outs = [
        (mine, swapped(mine)) for mine in (gains, w_key[0], w_value[0], w_query[0], w_out[0])
    ]

    mine = key_values(0, obs, gains, keys, values)

    def to_patch(value, steps):
        return {
            step: lax.ppermute(
                value, "patch", [(at, (at + step) % patch_count) for at in range(patch_count)]
            )
            for step in steps
        }

    arrived = to_patch(mine, (4, 3, 5)) | to_patch(mine, (2, 6, 1, 7))
    same = jnp.stack([mine] + [arrived[step] for step in range(1, patch_count)])
    kv_zero = (same, swapped(same))
    patch_group, mine = lax.optimization_barrier((patch_group, mine))
    patch_pieces = all_far(patch_group)
    mine = key_values(1, obs, gains, keys, values)

    def reduced(parts):
        arrived = {step: far(parts[step], step) for step in AROUND}
        return added(parts[0], [arrived[step] for step in range(1, SIDE)]).astype(jnp.bfloat16)

    *parts, kept = attend(0, lists, patch_pieces, kv_zero, gains, queries, outs)
    mine, _ = lax.optimization_barrier((mine, kept))
    arrived = to_patch(mine, (4, 1)) | to_patch(mine, (3, 5))
    arrived |= to_patch(mine, (2, 6, 7))
    same = jnp.stack([mine] + [arrived[step] for step in range(1, patch_count)])
    kv_one = (same, swapped(same))

    total = reduced(parts)
    first, *others = all_near(total)
    after_zero = (kept.astype(jnp.float32) + added(first, others)).astype(jnp.bfloat16)

    pieces = all_far(after_zero)
    own_zero = lax.dynamic_index_in_dim(after_zero, near_at, 0, keepdims=False)
    other_zero = swapped(own_zero)
    halves_zero = (
        jnp.where(core == 0, own_zero, other_zero),
        jnp.where(core == 0, other_zero, own_zero),
    )
    *parts, _ = attend(1, lists, pieces, kv_one, gains, queries, outs)
    total = reduced(parts)

    sent = lax.optimization_barrier(
        tuple(
            lax.dynamic_index_in_dim(total, wrapped(near_at + step), 0, keepdims=False)
            for step in range(SIDE)
        )
    )

    def to_last(core_from, step):
        pairs = [pair for pair in square_shift(True, step) if pair[0] // SIDE**2 == core_from]
        pairs = [(source, target % SIDE**2 + SIDE**2) for source, target in pairs]
        return lax.ppermute(sent[step], ("pipe", "obs"), pairs)

    own_total = sent[0]
    on_chip = to_last(0, 0)
    from_one = [to_last(1, step) for step in AROUND]
    from_zero = [on_chip] + [to_last(0, step) for step in AROUND]
    sums = (added(from_zero[0], from_zero[1:]), added(own_total, from_one))
    result = [
        jnp.where(
            core == 0, before, (before.astype(jnp.float32) + extra).astype(jnp.bfloat16)
        )
        for before, extra in zip(halves_zero, sums)
    ]
    return jnp.concatenate(result, axis=0)[None]


def solution(mesh):
    in_specs = (
        P("patch", "obs"),
        P("patch", "obs"),
        P("patch", None),
        P("patch"),
        P("patch", None),
        P("pipe", None, "obs"),
        P("pipe", None, "obs"),
        P("pipe", None, "obs"),
        P("pipe", "obs", None),
        P("pipe", None),
        P("pipe", None),
    )
    out_specs = P("pipe", "patch", "obs")
    return jax.shard_map(
        on_device, mesh=mesh, in_specs=in_specs, out_specs=out_specs, check_vma=False
    )
```

```python
import functools

import jax
import jax.numpy as jnp
from jax import lax
from jax.experimental import pallas as pl
from jax.experimental.pallas import tpu as pltpu
from jax.sharding import PartitionSpec as P


HS = 128
BLK = 128
SIDE = 4
EPS = 1e-05

SMEM = pl.BlockSpec(memory_space=pltpu.SMEM)
VMEM = pl.BlockSpec(memory_space=pltpu.VMEM)
ANY = pl.BlockSpec(memory_space=pl.ANY)
AROUND = (2, 1, 3)


def square_shift(first_axis, step):
    pairs = []
    for core in range(2):
        for row in range(SIDE):
            for col in range(SIDE):
                along_col = (core == 0) == first_axis
                new_row = row if along_col else (row + step) % SIDE
                new_col = (col + step) % SIDE if along_col else col
                base = core * SIDE * SIDE
                pairs.append((base + row * SIDE + col, base + new_row * SIDE + new_col))
    return pairs


def near(value, step):
    return lax.ppermute(value, ("pipe", "obs"), square_shift(True, step))


def far(value, step):
    return lax.ppermute(value, ("pipe", "obs"), square_shift(False, step))


def all_far(value):
    arrived = {step: far(value, step) for step in AROUND}
    return [value] + [arrived[step] for step in range(1, SIDE)]


def all_near(value):
    arrived = {step: near(value, step) for step in AROUND}
    return [value] + [arrived[step] for step in range(1, SIDE)]


def swapped(value):
    return lax.ppermute(value, "pipe", [(0, 1), (1, 0)])


def position():
    core = lax.axis_index("pipe")
    chip = lax.axis_index("obs")
    row = lax.div(chip, SIDE)
    col = lax.rem(chip, SIDE)
    near_at = jnp.where(core == 0, col, row)
    far_at = jnp.where(core == 0, row, col)
    near_stride = jnp.where(core == 0, 1, SIDE)
    far_stride = jnp.where(core == 0, SIDE, 1)
    return core, near_at, far_at, near_stride, far_stride


def wrapped(value):
    return lax.rem(value + SIDE, SIDE)


def tile_cols(block):
    return pl.ds(pl.multiple_of(block * HS, HS), HS)


def fetch(core, section, mine, theirs, target, sem, act):
    @pl.when(core == section)
    def _():
        act(pltpu.make_async_copy(mine, target, sem))

    @pl.when(core != section)
    def _():
        act(pltpu.make_async_copy(theirs, target, sem))


def start(copy):
    copy.start()


def wait(copy):
    copy.wait()


def placed(where, is_relative):
    _, near_at, far_at, near_stride, far_stride = where

    def block(step, part):
        at = wrapped(near_at - part) if is_relative else part
        return wrapped(far_at - step) * far_stride + at * near_stride

    return block


def normed_into(block_of, pieces, gain, normed):
    rows = normed.shape[0]

    def add_squares(part, squares):
        for piece in pieces:
            widened = piece[part].astype(jnp.float32)
            squares = squares + widened * widened
        return squares

    squares = lax.fori_loop(0, SIDE, add_squares, jnp.zeros((rows, HS), jnp.float32))
    mean = jnp.sum(squares, axis=-1, keepdims=True) * (1.0 / (SIDE * SIDE * HS))
    inverse = lax.rsqrt(mean + EPS)

    @pl.loop(0, SIDE)
    def _(part):
        for step, piece in enumerate(pieces):
            block = block_of(step, part)
            scaled = (piece[part].astype(jnp.float32) * inverse) * gain[pl.ds(block, 1), :]
            normed[:, tile_cols(block)] = scaled.astype(jnp.bfloat16)


def chosen_gain(core, section, mine, theirs, index, gain):
    gain[...] = jnp.where(core == section, mine[index], theirs[index])


def key_value_kernel(
    section,
    o0,
    o1,
    o2,
    o3,
    gain_mine,
    gain_theirs,
    key_mine,
    key_theirs,
    value_mine,
    value_theirs,
    out,
    normed,
    weight,
    gain,
    sems,
):
    where = position()
    core = where[0]
    key_at, value_at = weight.at[:, :HS], weight.at[:, HS:]
    fetch(core, section, key_mine, key_theirs, key_at, sems.at[0], start)
    fetch(core, section, value_mine, value_theirs, value_at, sems.at[1], start)
    chosen_gain(core, section, gain_mine, gain_theirs, 1, gain)
    normed_into(placed(where, True), (o0, o1, o2, o3), gain, normed)
    fetch(core, section, key_mine, key_theirs, key_at, sems.at[0], wait)
    fetch(core, section, value_mine, value_theirs, value_at, sems.at[1], wait)
    out[...] = jnp.dot(
        normed[...], weight[...], preferred_element_type=jnp.float32
    ).astype(jnp.bfloat16)


def attend_kernel(
    section,
    entries,
    counts,
    bias,
    x0,
    x1,
    x2,
    x3,
    kv_same,
    kv_other,
    gain_mine,
    gain_theirs,
    query_mine,
    query_theirs,
    out_mine,
    out_theirs,
    y0,
    y1,
    y2,
    y3,
    kept,
    normed,
    context,
    w_query,
    w_out,
    gain,
    sems,
):
    rows = normed.shape[0]
    slots = entries.shape[1]
    where = position()
    core, near_at, far_at, near_stride, far_stride = where
    place = lax.axis_index("patch")
    patch_count = kv_same.shape[0]
    fetch(core, section, query_mine, query_theirs, w_query, sems.at[0], start)
    fetch(core, section, out_mine, out_theirs, w_out, sems.at[1], start)
    chosen_gain(core, section, gain_mine, gain_theirs, 0, gain)
    normed_into(placed(where, section == 0), (x0, x1, x2, x3), gain, normed)
    if section == 0:

        @pl.loop(0, SIDE)
        def _(part):
            kept[part] = x0[wrapped(near_at - part)]

    fetch(core, section, query_mine, query_theirs, w_query, sems.at[0], wait)
    context[...] = (
        jnp.dot(normed[...], w_query[...], preferred_element_type=jnp.float32) * HS ** (-0.5)
    ).astype(jnp.bfloat16)
    blocks_here = rows // BLK

    @pl.loop(0, blocks_here)
    def _(block):
        here = pl.ds(pl.multiple_of(block * BLK, BLK), BLK)
        query = context[here, :]
        row = core * blocks_here + block
        live = counts[row]
        scores, values = [], []
        for slot in range(slots):
            entry = jnp.where(slot < live, entries[row, slot], 0)
            owner = lax.div(entry, 2)
            index = lax.rem(place - owner + patch_count, patch_count)
            is_same = (entry - owner * 2) == core
            both = jnp.where(is_same, kv_same[index], kv_other[index])
            score = lax.dot_general(
                query,
                both[:, :HS],
                (((1,), (1,)), ((), ())),
                preferred_element_type=jnp.float32,
            )
            scores.append(jnp.where(slot < live, score + bias[row, slot], -1e30))
            values.append(both[:, HS:])
        scores = jnp.concatenate(scores, axis=1)
        top = jnp.max(scores, axis=-1, keepdims=True)
        weights = jnp.exp(scores - top)
        weights = (weights * (1.0 / jnp.sum(weights, axis=-1, keepdims=True))).astype(jnp.bfloat16)
        context[here, :] = jnp.dot(
            weights, jnp.concatenate(values, axis=0), preferred_element_type=jnp.float32
        ).astype(jnp.bfloat16)

    fetch(core, section, out_mine, out_theirs, w_out, sems.at[1], wait)
    ready = context[...]
    width = SIDE * HS

    @pl.loop(0, SIDE)
    def _(part):
        cols = pl.ds(pl.multiple_of(part * width, width), width)
        normed[:, cols] = jnp.dot(
            ready, w_out[:, cols], preferred_element_type=jnp.float32
        ).astype(jnp.bfloat16)

    @pl.loop(0, SIDE)
    def _(part):
        for step, out in enumerate((y0, y1, y2, y3)):
            block = wrapped(far_at + step) * far_stride + part * near_stride
            out[part] = normed[:, tile_cols(block)]


def key_values(section, pieces, gains, w_key, w_value):
    rows = pieces[0].shape[1]
    features = w_key[0].shape[0]
    return pl.pallas_call(
        functools.partial(key_value_kernel, section),
        out_shape=jax.ShapeDtypeStruct((rows, 2 * HS), jnp.bfloat16),
        in_specs=[VMEM] * 6 + [ANY] * 4,
        out_specs=VMEM,
        scratch_shapes=[
            pltpu.VMEM((rows, features), jnp.bfloat16),
            pltpu.VMEM((features, 2 * HS), jnp.bfloat16),
            pltpu.VMEM(gains[0].shape[1:], jnp.float32),
            pltpu.SemaphoreType.DMA((2,)),
        ],
        cost_estimate=pl.CostEstimate(
            flops=4 * rows * features * HS, bytes_accessed=6 * features * HS, transcendentals=0
        ),
        compiler_params=pltpu.CompilerParams(vmem_limit_bytes=8 << 20),
        name="key_values",
    )(*pieces, *gains, *w_key, *w_value)


def attend(section, lists, pieces, kv, gains, w_query, w_out):
    rows = pieces[0].shape[1]
    features = w_query[0].shape[0]
    piece = jax.ShapeDtypeStruct((SIDE, rows, HS), jnp.bfloat16)
    extra = piece if section == 0 else jax.ShapeDtypeStruct((8, HS), jnp.bfloat16)
    return pl.pallas_call(
        functools.partial(attend_kernel, section),
        out_shape=[piece] * SIDE + [extra],
        in_specs=[SMEM] * 3 + [VMEM] * 8 + [ANY] * 4,
        out_specs=[VMEM] * 5,
        scratch_shapes=[
            pltpu.VMEM((rows, features), jnp.bfloat16),
            pltpu.VMEM((rows, HS), jnp.bfloat16),
            pltpu.VMEM(w_query[0].shape, jnp.bfloat16),
            pltpu.VMEM(w_out[0].shape, jnp.bfloat16),
            pltpu.VMEM(gains[0].shape[1:], jnp.float32),
            pltpu.SemaphoreType.DMA((2,)),
        ],
        cost_estimate=pl.CostEstimate(
            flops=8 * rows * features * HS,
            bytes_accessed=16 * features * HS,
            transcendentals=rows * 1024,
        ),
        compiler_params=pltpu.CompilerParams(vmem_limit_bytes=12 << 20),
        name="attend",
    )(*lists, *pieces, *kv, *gains, *w_query, *w_out)


def added(first, others):
    total = first.astype(jnp.float32)
    for other in others:
        total = total + other.astype(jnp.float32)
    return total


def on_device(
    patch_tokens,
    obs_tokens,
    footprint,
    list_counts,
    footprint_bias,
    w_query,
    w_key,
    w_value,
    w_out,
    patch_gain,
    obs_gain,
):
    core, near_at, _, _, _ = position()
    patch_count = lax.axis_size("patch")
    patch_rows = patch_tokens.shape[0] // 2
    obs_rows = obs_tokens.shape[0] // 2
    lists = (footprint, list_counts, footprint_bias)

    my_obs = lax.dynamic_slice_in_dim(obs_tokens, core * obs_rows, obs_rows, 0)
    my_patch = lax.dynamic_slice_in_dim(patch_tokens, core * patch_rows, patch_rows, 0)
    group = jnp.stack(all_near(jnp.concatenate([my_obs, my_patch], axis=0)))
    obs_group, patch_group = group[:, :obs_rows], group[:, obs_rows:]

    gains = jnp.concatenate([patch_gain, obs_gain], axis=0).reshape(2, SIDE * SIDE, HS)
    gains, keys, values, queries, outs = [
        (mine, swapped(mine)) for mine in (gains, w_key[0], w_value[0], w_query[0], w_out[0])
    ]

    obs_pieces = all_far(obs_group)
    mine = key_values(0, obs_pieces, gains, keys, values)

    def to_patch(value, steps):
        return {
            step: lax.ppermute(
                value, "patch", [(at, (at + step) % patch_count) for at in range(patch_count)]
            )
            for step in steps
        }

    arrived = to_patch(mine, (4, 3, 5)) | to_patch(mine, (2, 6, 1, 7))
    same = jnp.stack([mine] + [arrived[step] for step in range(1, patch_count)])
    kv_zero = (same, swapped(same))
    patch_group, mine = lax.optimization_barrier((patch_group, mine))
    patch_pieces = all_far(patch_group)
    mine = key_values(1, obs_pieces, gains, keys, values)

    def reduced(parts):
        arrived = {step: far(parts[step], step) for step in AROUND}
        return added(parts[0], [arrived[step] for step in range(1, SIDE)]).astype(jnp.bfloat16)

    *parts, kept = attend(0, lists, patch_pieces, kv_zero, gains, queries, outs)
    mine, _ = lax.optimization_barrier((mine, kept))
    arrived = to_patch(mine, (4, 1)) | to_patch(mine, (3, 5))
    arrived |= to_patch(mine, (2, 6, 7))
    same = jnp.stack([mine] + [arrived[step] for step in range(1, patch_count)])
    kv_one = (same, swapped(same))

    total = reduced(parts)
    first, *others = all_near(total)
    after_zero = (kept.astype(jnp.float32) + added(first, others)).astype(jnp.bfloat16)

    pieces = all_far(after_zero)
    *parts, _ = attend(1, lists, pieces, kv_one, gains, queries, outs)
    total = reduced(parts)
    own_zero = lax.dynamic_index_in_dim(after_zero, near_at, 0, keepdims=False)
    own_total = lax.dynamic_index_in_dim(total, near_at, 0, keepdims=False)
    others = [
        near(lax.dynamic_index_in_dim(total, wrapped(near_at + step), 0, keepdims=False), step)
        for step in AROUND
    ]
    own_one = (own_zero.astype(jnp.float32) + added(own_total, others)).astype(jnp.bfloat16)

    arrived = swapped(jnp.where(core == 0, own_one, own_zero))
    upper = jnp.where(core == 0, own_zero, arrived)
    lower = jnp.where(core == 0, arrived, own_one)
    return jnp.concatenate([upper, lower], axis=0)[None]


def solution(mesh):
    in_specs = (
        P("patch", "obs"),
        P("patch", "obs"),
        P("patch", None),
        P("patch"),
        P("patch", None),
        P("pipe", None, "obs"),
        P("pipe", None, "obs"),
        P("pipe", None, "obs"),
        P("pipe", "obs", None),
        P("pipe", None),
        P("pipe", None),
    )
    out_specs = P("pipe", "patch", "obs")
    return jax.shard_map(
        on_device, mesh=mesh, in_specs=in_specs, out_specs=out_specs, check_vma=False
    )
```

```python
import functools

import jax
import jax.numpy as jnp
from jax import lax
from jax.experimental import pallas as pl
from jax.experimental.pallas import tpu as pltpu
from jax.sharding import PartitionSpec as P


HS = 128
BLK = 128
SIDE = 4
EPS = 1e-05

SMEM = pl.BlockSpec(memory_space=pltpu.SMEM)
VMEM = pl.BlockSpec(memory_space=pltpu.VMEM)
ANY = pl.BlockSpec(memory_space=pl.ANY)
AROUND = (2, 1, 3)


def square_shift(first_axis, step):
    pairs = []
    for core in range(2):
        for row in range(SIDE):
            for col in range(SIDE):
                along_col = (core == 0) == first_axis
                new_row = row if along_col else (row + step) % SIDE
                new_col = (col + step) % SIDE if along_col else col
                base = core * SIDE * SIDE
                pairs.append((base + row * SIDE + col, base + new_row * SIDE + new_col))
    return pairs


def near(value, step):
    return lax.ppermute(value, ("pipe", "obs"), square_shift(True, step))


def far(value, step):
    return lax.ppermute(value, ("pipe", "obs"), square_shift(False, step))


def all_far(value):
    arrived = {step: far(value, step) for step in AROUND}
    return [value] + [arrived[step] for step in range(1, SIDE)]


def all_near(value):
    arrived = {step: near(value, step) for step in AROUND}
    return [value] + [arrived[step] for step in range(1, SIDE)]


def swapped(value):
    return lax.ppermute(value, "pipe", [(0, 1), (1, 0)])


def position():
    core = lax.axis_index("pipe")
    chip = lax.axis_index("obs")
    row = lax.div(chip, SIDE)
    col = lax.rem(chip, SIDE)
    near_at = jnp.where(core == 0, col, row)
    far_at = jnp.where(core == 0, row, col)
    near_stride = jnp.where(core == 0, 1, SIDE)
    far_stride = jnp.where(core == 0, SIDE, 1)
    return core, near_at, far_at, near_stride, far_stride


def wrapped(value):
    return lax.rem(value + SIDE, SIDE)


def tile_cols(block):
    return pl.ds(pl.multiple_of(block * HS, HS), HS)


def fetch(core, section, mine, theirs, target, sem, act):
    @pl.when(core == section)
    def _():
        act(pltpu.make_async_copy(mine, target, sem))

    @pl.when(core != section)
    def _():
        act(pltpu.make_async_copy(theirs, target, sem))


def start(copy):
    copy.start()


def wait(copy):
    copy.wait()


def placed(where, is_relative):
    _, near_at, far_at, near_stride, far_stride = where

    def block(step, part):
        at = wrapped(near_at - part) if is_relative else part
        return wrapped(far_at - step) * far_stride + at * near_stride

    return block


def normed_into(block_of, pieces, gains, targets):
    rows = targets[0].shape[0]

    def add_squares(part, squares):
        for piece in pieces:
            widened = piece[part].astype(jnp.float32)
            squares = squares + widened * widened
        return squares

    squares = lax.fori_loop(0, SIDE, add_squares, jnp.zeros((rows, HS), jnp.float32))
    mean = jnp.sum(squares, axis=-1, keepdims=True) * (1.0 / (SIDE * SIDE * HS))
    inverse = lax.rsqrt(mean + EPS)

    @pl.loop(0, SIDE)
    def _(part):
        for step, piece in enumerate(pieces):
            block = block_of(step, part)
            scaled = piece[part].astype(jnp.float32) * inverse
            for gain, target in zip(gains, targets):
                target[:, tile_cols(block)] = (scaled * gain[pl.ds(block, 1), :]).astype(
                    jnp.bfloat16
                )


def chosen_gain(core, section, mine, theirs, index, gain):
    gain[...] = jnp.where(core == section, mine[index], theirs[index])


def key_value_kernel(
    o0,
    o1,
    o2,
    o3,
    gain_mine,
    gain_theirs,
    key_mine,
    key_theirs,
    value_mine,
    value_theirs,
    out_zero,
    out_one,
    normed,
    weight,
    sems,
):
    sources = ((key_mine, value_mine), (key_theirs, value_theirs))
    copies = [
        pltpu.make_async_copy(
            source, weight.at[whose, :, half * HS : (half + 1) * HS], sems.at[whose * 2 + half]
        )
        for whose, pair in enumerate(sources)
        for half, source in enumerate(pair)
    ]
    for copy in copies:
        copy.start()
    gains = (gain_mine.at[1], gain_theirs.at[1])
    targets = (normed.at[0], normed.at[1])
    where = position()
    normed_into(placed(where, True), (o0, o1, o2, o3), gains, targets)
    for copy in copies:
        copy.wait()
    for section, out in enumerate((out_zero, out_one)):
        whose = lax.rem(where[0] + section, 2)
        out[...] = jnp.dot(
            normed[whose], weight[whose], preferred_element_type=jnp.float32
        ).astype(jnp.bfloat16)


def attend_kernel(
    section,
    entries,
    counts,
    bias,
    x0,
    x1,
    x2,
    x3,
    kv_same,
    kv_other,
    gain_mine,
    gain_theirs,
    query_mine,
    query_theirs,
    out_mine,
    out_theirs,
    y0,
    y1,
    y2,
    y3,
    kept,
    normed,
    context,
    w_query,
    w_out,
    gain,
    sems,
):
    rows = normed.shape[0]
    slots = entries.shape[1]
    where = position()
    core, near_at, far_at, near_stride, far_stride = where
    place = lax.axis_index("patch")
    patch_count = kv_same.shape[0]
    fetch(core, section, query_mine, query_theirs, w_query, sems.at[0], start)
    fetch(core, section, out_mine, out_theirs, w_out, sems.at[1], start)
    chosen_gain(core, section, gain_mine, gain_theirs, 0, gain)
    normed_into(placed(where, section == 0), (x0, x1, x2, x3), (gain,), (normed,))
    if section == 0:

        @pl.loop(0, SIDE)
        def _(part):
            kept[part] = x0[wrapped(near_at - part)]

    fetch(core, section, query_mine, query_theirs, w_query, sems.at[0], wait)
    context[...] = (
        jnp.dot(normed[...], w_query[...], preferred_element_type=jnp.float32) * HS ** (-0.5)
    ).astype(jnp.bfloat16)
    blocks_here = rows // BLK

    @pl.loop(0, blocks_here)
    def _(block):
        here = pl.ds(pl.multiple_of(block * BLK, BLK), BLK)
        query = context[here, :]
        row = core * blocks_here + block
        live = counts[row]
        scores, values = [], []
        for slot in range(slots):
            entry = jnp.where(slot < live, entries[row, slot], 0)
            owner = lax.div(entry, 2)
            index = lax.rem(place - owner + patch_count, patch_count)
            is_same = (entry - owner * 2) == core
            both = jnp.where(is_same, kv_same[index], kv_other[index])
            score = lax.dot_general(
                query,
                both[:, :HS],
                (((1,), (1,)), ((), ())),
                preferred_element_type=jnp.float32,
            )
            scores.append(jnp.where(slot < live, score + bias[row, slot], -1e30))
            values.append(both[:, HS:])
        scores = jnp.concatenate(scores, axis=1)
        top = jnp.max(scores, axis=-1, keepdims=True)
        weights = jnp.exp(scores - top)
        weights = (weights * (1.0 / jnp.sum(weights, axis=-1, keepdims=True))).astype(jnp.bfloat16)
        context[here, :] = jnp.dot(
            weights, jnp.concatenate(values, axis=0), preferred_element_type=jnp.float32
        ).astype(jnp.bfloat16)

    fetch(core, section, out_mine, out_theirs, w_out, sems.at[1], wait)
    ready = context[...]
    width = SIDE * HS

    @pl.loop(0, SIDE)
    def _(part):
        cols = pl.ds(pl.multiple_of(part * width, width), width)
        normed[:, cols] = jnp.dot(
            ready, w_out[:, cols], preferred_element_type=jnp.float32
        ).astype(jnp.bfloat16)

    @pl.loop(0, SIDE)
    def _(part):
        for step, out in enumerate((y0, y1, y2, y3)):
            block = wrapped(far_at + step) * far_stride + part * near_stride
            out[part] = normed[:, tile_cols(block)]


def key_values(pieces, gains, w_key, w_value):
    rows = pieces[0].shape[1]
    features = w_key[0].shape[0]
    return pl.pallas_call(
        key_value_kernel,
        out_shape=[jax.ShapeDtypeStruct((rows, 2 * HS), jnp.bfloat16)] * 2,
        in_specs=[VMEM] * 6 + [ANY] * 4,
        out_specs=[VMEM] * 2,
        scratch_shapes=[
            pltpu.VMEM((2, rows, features), jnp.bfloat16),
            pltpu.VMEM((2, features, 2 * HS), jnp.bfloat16),
            pltpu.SemaphoreType.DMA((4,)),
        ],
        cost_estimate=pl.CostEstimate(
            flops=8 * rows * features * HS, bytes_accessed=10 * features * HS, transcendentals=0
        ),
        compiler_params=pltpu.CompilerParams(vmem_limit_bytes=12 << 20),
        name="key_values",
    )(*pieces, *gains, *w_key, *w_value)


def attend(section, lists, pieces, kv, gains, w_query, w_out):
    rows = pieces[0].shape[1]
    features = w_query[0].shape[0]
    piece = jax.ShapeDtypeStruct((SIDE, rows, HS), jnp.bfloat16)
    extra = piece if section == 0 else jax.ShapeDtypeStruct((8, HS), jnp.bfloat16)
    return pl.pallas_call(
        functools.partial(attend_kernel, section),
        out_shape=[piece] * SIDE + [extra],
        in_specs=[SMEM] * 3 + [VMEM] * 8 + [ANY] * 4,
        out_specs=[VMEM] * 5,
        scratch_shapes=[
            pltpu.VMEM((rows, features), jnp.bfloat16),
            pltpu.VMEM((rows, HS), jnp.bfloat16),
            pltpu.VMEM(w_query[0].shape, jnp.bfloat16),
            pltpu.VMEM(w_out[0].shape, jnp.bfloat16),
            pltpu.VMEM(gains[0].shape[1:], jnp.float32),
            pltpu.SemaphoreType.DMA((2,)),
        ],
        cost_estimate=pl.CostEstimate(
            flops=8 * rows * features * HS,
            bytes_accessed=16 * features * HS,
            transcendentals=rows * 1024,
        ),
        compiler_params=pltpu.CompilerParams(vmem_limit_bytes=12 << 20),
        name="attend",
    )(*lists, *pieces, *kv, *gains, *w_query, *w_out)


def added(first, others):
    total = first.astype(jnp.float32)
    for other in others:
        total = total + other.astype(jnp.float32)
    return total


def on_device(
    patch_tokens,
    obs_tokens,
    footprint,
    list_counts,
    footprint_bias,
    w_query,
    w_key,
    w_value,
    w_out,
    patch_gain,
    obs_gain,
):
    core, near_at, _, _, _ = position()
    patch_count = lax.axis_size("patch")
    patch_rows = patch_tokens.shape[0] // 2
    obs_rows = obs_tokens.shape[0] // 2
    lists = (footprint, list_counts, footprint_bias)

    my_obs = lax.dynamic_slice_in_dim(obs_tokens, core * obs_rows, obs_rows, 0)
    my_patch = lax.dynamic_slice_in_dim(patch_tokens, core * patch_rows, patch_rows, 0)
    group = jnp.stack(all_near(jnp.concatenate([my_obs, my_patch], axis=0)))
    obs_group, patch_group = group[:, :obs_rows], group[:, obs_rows:]

    gains = jnp.concatenate([patch_gain, obs_gain], axis=0).reshape(2, SIDE * SIDE, HS)
    gains, keys, values = [(mine, swapped(mine)) for mine in (gains, w_key[0], w_value[0])]
    queries, outs = [(mine, swapped(mine)) for mine in (w_query[0], w_out[0])]

    obs_far = {}
    for step in AROUND:
        obs_far[step] = far(obs_group, step)
    obs_pieces = [obs_group] + [obs_far[step] for step in range(1, SIDE)]
    kv_first, kv_second = key_values(obs_pieces, gains, keys, values)

    def to_patch(value, steps):
        return {
            step: lax.ppermute(
                value, "patch", [(at, (at + step) % patch_count) for at in range(patch_count)]
            )
            for step in steps
        }

    arrived = to_patch(kv_first, (4, 3, 5)) | to_patch(kv_first, (2, 6, 1, 7))
    same = jnp.stack([kv_first] + [arrived[step] for step in range(1, patch_count)])
    kv_zero = (same, swapped(same))
    patch_pieces = all_far(patch_group)

    def reduced(parts):
        arrived = {step: far(parts[step], step) for step in AROUND}
        return added(parts[0], [arrived[step] for step in range(1, SIDE)]).astype(jnp.bfloat16)

    *parts, kept = attend(0, lists, patch_pieces, kv_zero, gains, queries, outs)
    kv_second, _ = lax.optimization_barrier((kv_second, kept))
    arrived = to_patch(kv_second, (1, 7)) | to_patch(kv_second, (4, 3, 5))
    arrived |= to_patch(kv_second, (2, 6))
    same = jnp.stack([kv_second] + [arrived[step] for step in range(1, patch_count)])
    kv_one = (same, swapped(same))

    total = reduced(parts)
    first, *others = all_near(total)
    after_zero = (kept.astype(jnp.float32) + added(first, others)).astype(jnp.bfloat16)

    pieces = all_far(after_zero)
    *parts, _ = attend(1, lists, pieces, kv_one, gains, queries, outs)
    total = reduced(parts)
    own_zero = lax.dynamic_index_in_dim(after_zero, near_at, 0, keepdims=False)
    own_total = lax.dynamic_index_in_dim(total, near_at, 0, keepdims=False)
    others = [
        near(lax.dynamic_index_in_dim(total, wrapped(near_at + step), 0, keepdims=False), step)
        for step in AROUND
    ]
    own_one = (own_zero.astype(jnp.float32) + added(own_total, others)).astype(jnp.bfloat16)

    arrived = swapped(jnp.where(core == 0, own_one, own_zero))
    upper = jnp.where(core == 0, own_zero, arrived)
    lower = jnp.where(core == 0, arrived, own_one)
    return jnp.concatenate([upper, lower], axis=0)[None]


def solution(mesh):
    in_specs = (
        P("patch", "obs"),
        P("patch", "obs"),
        P("patch", None),
        P("patch"),
        P("patch", None),
        P("pipe", None, "obs"),
        P("pipe", None, "obs"),
        P("pipe", None, "obs"),
        P("pipe", "obs", None),
        P("pipe", None),
        P("pipe", None),
    )
    out_specs = P("pipe", "patch", "obs")
    return jax.shard_map(
        on_device, mesh=mesh, in_specs=in_specs, out_specs=out_specs, check_vma=False
    )
```

```python
import functools

import jax
import jax.numpy as jnp
from jax import lax
from jax.experimental import pallas as pl
from jax.experimental.pallas import tpu as pltpu
from jax.sharding import PartitionSpec as P


HS = 128
BLK = 128
SIDE = 4
EPS = 1e-05

SMEM = pl.BlockSpec(memory_space=pltpu.SMEM)
VMEM = pl.BlockSpec(memory_space=pltpu.VMEM)
ANY = pl.BlockSpec(memory_space=pl.ANY)
AROUND = (2, 1, 3)


def square_shift(first_axis, step):
    pairs = []
    for core in range(2):
        for row in range(SIDE):
            for col in range(SIDE):
                along_col = (core == 0) == first_axis
                new_row = row if along_col else (row + step) % SIDE
                new_col = (col + step) % SIDE if along_col else col
                base = core * SIDE * SIDE
                pairs.append((base + row * SIDE + col, base + new_row * SIDE + new_col))
    return pairs


def near(value, step):
    return lax.ppermute(value, ("pipe", "obs"), square_shift(True, step))


def far(value, step):
    return lax.ppermute(value, ("pipe", "obs"), square_shift(False, step))


def all_far(value):
    arrived = {step: far(value, step) for step in AROUND}
    return [value] + [arrived[step] for step in range(1, SIDE)]


def all_near(value):
    arrived = {step: near(value, step) for step in AROUND}
    return [value] + [arrived[step] for step in range(1, SIDE)]


def swapped(value):
    return lax.ppermute(value, "pipe", [(0, 1), (1, 0)])


def position():
    core = lax.axis_index("pipe")
    chip = lax.axis_index("obs")
    row = lax.div(chip, SIDE)
    col = lax.rem(chip, SIDE)
    near_at = jnp.where(core == 0, col, row)
    far_at = jnp.where(core == 0, row, col)
    near_stride = jnp.where(core == 0, 1, SIDE)
    far_stride = jnp.where(core == 0, SIDE, 1)
    return core, near_at, far_at, near_stride, far_stride


def wrapped(value):
    return lax.rem(value + SIDE, SIDE)


def tile_cols(block):
    return pl.ds(pl.multiple_of(block * HS, HS), HS)


def fetch(core, section, mine, theirs, target, sem, act):
    @pl.when(core == section)
    def _():
        act(pltpu.make_async_copy(mine, target, sem))

    @pl.when(core != section)
    def _():
        act(pltpu.make_async_copy(theirs, target, sem))


def start(copy):
    copy.start()


def wait(copy):
    copy.wait()


def placed(where, is_relative):
    _, near_at, far_at, near_stride, far_stride = where

    def block(step, part):
        at = wrapped(near_at - part) if is_relative else part
        return wrapped(far_at - step) * far_stride + at * near_stride

    return block


def normed_into(block_of, pieces, gains, targets):
    rows = targets[0].shape[0]

    def add_squares(part, squares):
        for piece in pieces:
            widened = piece[part].astype(jnp.float32)
            squares = squares + widened * widened
        return squares

    squares = lax.fori_loop(0, SIDE, add_squares, jnp.zeros((rows, HS), jnp.float32))
    mean = jnp.sum(squares, axis=-1, keepdims=True) * (1.0 / (SIDE * SIDE * HS))
    inverse = lax.rsqrt(mean + EPS)

    @pl.loop(0, SIDE)
    def _(part):
        for step, piece in enumerate(pieces):
            block = block_of(step, part)
            scaled = piece[part].astype(jnp.float32) * inverse
            for gain, target in zip(gains, targets):
                target[:, tile_cols(block)] = (scaled * gain[pl.ds(block, 1), :]).astype(
                    jnp.bfloat16
                )


def chosen_gain(core, section, mine, theirs, index, gain):
    gain[...] = jnp.where(core == section, mine[index], theirs[index])


def key_value_kernel(
    o0,
    o1,
    o2,
    o3,
    gain_mine,
    gain_theirs,
    key_mine,
    value_mine,
    theirs,
    out_zero,
    out_one,
    normed,
    weight,
    sems,
):
    sources = ((key_mine, value_mine), (theirs.at[0], theirs.at[1]))
    copies = [
        pltpu.make_async_copy(
            source, weight.at[whose, :, half * HS : (half + 1) * HS], sems.at[whose * 2 + half]
        )
        for whose, pair in enumerate(sources)
        for half, source in enumerate(pair)
    ]
    for copy in copies:
        copy.start()
    gains = (gain_mine.at[1], gain_theirs.at[1])
    targets = (normed.at[0], normed.at[1])
    where = position()
    normed_into(placed(where, True), (o0, o1, o2, o3), gains, targets)
    for copy in copies:
        copy.wait()
    for section, out in enumerate((out_zero, out_one)):
        whose = lax.rem(where[0] + section, 2)
        out[...] = jnp.dot(
            normed[whose], weight[whose], preferred_element_type=jnp.float32
        ).astype(jnp.bfloat16)


def attend_kernel(
    section,
    entries,
    counts,
    bias,
    x0,
    x1,
    x2,
    x3,
    kv_same,
    kv_other,
    gain_mine,
    gain_theirs,
    query_mine,
    query_theirs,
    out_mine,
    out_theirs,
    y0,
    y1,
    y2,
    y3,
    kept,
    normed,
    context,
    w_query,
    w_out,
    gain,
    sems,
):
    rows = normed.shape[0]
    slots = entries.shape[1]
    where = position()
    core, near_at, far_at, near_stride, far_stride = where
    place = lax.axis_index("patch")
    patch_count = kv_same.shape[0]
    fetch(core, section, query_mine, query_theirs.at[2], w_query, sems.at[0], start)
    fetch(core, section, out_mine, out_theirs, w_out, sems.at[1], start)
    chosen_gain(core, section, gain_mine, gain_theirs, 0, gain)
    normed_into(placed(where, section == 0), (x0, x1, x2, x3), (gain,), (normed,))
    if section == 0:

        @pl.loop(0, SIDE)
        def _(part):
            kept[part] = x0[wrapped(near_at - part)]

    fetch(core, section, query_mine, query_theirs.at[2], w_query, sems.at[0], wait)
    context[...] = (
        jnp.dot(normed[...], w_query[...], preferred_element_type=jnp.float32) * HS ** (-0.5)
    ).astype(jnp.bfloat16)
    blocks_here = rows // BLK

    for block in range(blocks_here):
        here = slice(block * BLK, (block + 1) * BLK)
        query = context[here, :]
        row = core * blocks_here + block
        live = counts[row]
        scores, values = [], []
        for slot in range(slots):
            entry = jnp.where(slot < live, entries[row, slot], 0)
            owner = lax.div(entry, 2)
            index = lax.rem(place - owner + patch_count, patch_count)
            is_same = (entry - owner * 2) == core
            both = jnp.where(is_same, kv_same[index], kv_other[index])
            score = lax.dot_general(
                query,
                both[:, :HS],
                (((1,), (1,)), ((), ())),
                preferred_element_type=jnp.float32,
            )
            scores.append(jnp.where(slot < live, score + bias[row, slot], -1e30))
            values.append(both[:, HS:])
        scores = jnp.concatenate(scores, axis=1)
        top = jnp.max(scores, axis=-1, keepdims=True)
        weights = jnp.exp(scores - top)
        weights = (weights * (1.0 / jnp.sum(weights, axis=-1, keepdims=True))).astype(jnp.bfloat16)
        context[here, :] = jnp.dot(
            weights, jnp.concatenate(values, axis=0), preferred_element_type=jnp.float32
        ).astype(jnp.bfloat16)

    fetch(core, section, out_mine, out_theirs, w_out, sems.at[1], wait)
    ready = context[...]
    width = SIDE * HS

    @pl.loop(0, SIDE)
    def _(part):
        cols = pl.ds(pl.multiple_of(part * width, width), width)
        normed[:, cols] = jnp.dot(
            ready, w_out[:, cols], preferred_element_type=jnp.float32
        ).astype(jnp.bfloat16)

    @pl.loop(0, SIDE)
    def _(part):
        for step, out in enumerate((y0, y1, y2, y3)):
            block = wrapped(far_at + step) * far_stride + part * near_stride
            out[part] = normed[:, tile_cols(block)]


def key_values(pieces, gains, weights):
    rows = pieces[0].shape[1]
    features = weights[0].shape[0]
    return pl.pallas_call(
        key_value_kernel,
        out_shape=[jax.ShapeDtypeStruct((rows, 2 * HS), jnp.bfloat16)] * 2,
        in_specs=[VMEM] * 6 + [ANY] * 3,
        out_specs=[VMEM] * 2,
        scratch_shapes=[
            pltpu.VMEM((2, rows, features), jnp.bfloat16),
            pltpu.VMEM((2, features, 2 * HS), jnp.bfloat16),
            pltpu.SemaphoreType.DMA((4,)),
        ],
        cost_estimate=pl.CostEstimate(
            flops=8 * rows * features * HS, bytes_accessed=10 * features * HS, transcendentals=0
        ),
        compiler_params=pltpu.CompilerParams(vmem_limit_bytes=12 << 20),
        name="key_values",
    )(*pieces, *gains, *weights)


def attend(section, lists, pieces, kv, gains, w_query, w_out):
    rows = pieces[0].shape[1]
    features = w_query[0].shape[0]
    piece = jax.ShapeDtypeStruct((SIDE, rows, HS), jnp.bfloat16)
    extra = piece if section == 0 else jax.ShapeDtypeStruct((8, HS), jnp.bfloat16)
    return pl.pallas_call(
        functools.partial(attend_kernel, section),
        out_shape=[piece] * SIDE + [extra],
        in_specs=[SMEM] * 3 + [VMEM] * 8 + [ANY] * 4,
        out_specs=[VMEM] * 5,
        scratch_shapes=[
            pltpu.VMEM((rows, features), jnp.bfloat16),
            pltpu.VMEM((rows, HS), jnp.bfloat16),
            pltpu.VMEM(w_query[0].shape, jnp.bfloat16),
            pltpu.VMEM(w_out[0].shape, jnp.bfloat16),
            pltpu.VMEM(gains[0].shape[1:], jnp.float32),
            pltpu.SemaphoreType.DMA((2,)),
        ],
        cost_estimate=pl.CostEstimate(
            flops=8 * rows * features * HS,
            bytes_accessed=16 * features * HS,
            transcendentals=rows * 1024,
        ),
        compiler_params=pltpu.CompilerParams(vmem_limit_bytes=12 << 20),
        name="attend",
    )(*lists, *pieces, *kv, *gains, *w_query, *w_out)


def added(first, others):
    total = first.astype(jnp.float32)
    for other in others:
        total = total + other.astype(jnp.float32)
    return total


def on_device(
    patch_tokens,
    obs_tokens,
    footprint,
    list_counts,
    footprint_bias,
    w_query,
    w_key,
    w_value,
    w_out,
    patch_gain,
    obs_gain,
):
    core, near_at, _, _, _ = position()
    patch_count = lax.axis_size("patch")
    patch_rows = patch_tokens.shape[0] // 2
    obs_rows = obs_tokens.shape[0] // 2
    lists = (footprint, list_counts, footprint_bias)

    my_obs = lax.dynamic_slice_in_dim(obs_tokens, core * obs_rows, obs_rows, 0)
    my_patch = lax.dynamic_slice_in_dim(patch_tokens, core * patch_rows, patch_rows, 0)
    group = jnp.stack(all_near(jnp.concatenate([my_obs, my_patch], axis=0)))
    obs_group, patch_group = group[:, :obs_rows], group[:, obs_rows:]

    gains = jnp.concatenate([patch_gain, obs_gain], axis=0).reshape(2, SIDE * SIDE, HS)
    gains = (gains, swapped(gains))
    theirs = swapped(jnp.stack([w_key[0], w_value[0], w_query[0]]))
    outs = (w_out[0], swapped(w_out[0]))

    obs_far = {}
    for step in AROUND:
        obs_far[step] = far(obs_group, step)
    obs_pieces = [obs_group] + [obs_far[step] for step in range(1, SIDE)]
    kv_first, kv_second = key_values(obs_pieces, gains, (w_key[0], w_value[0], theirs))

    def to_patch(value, steps):
        return {
            step: lax.ppermute(
                value, "patch", [(at, (at + step) % patch_count) for at in range(patch_count)]
            )
            for step in steps
        }

    arrived = to_patch(kv_first, (4, 3, 5)) | to_patch(kv_first, (2, 6, 1, 7))
    same = jnp.stack([kv_first] + [arrived[step] for step in range(1, patch_count)])
    kv_zero = (same, swapped(same))
    patch_pieces = all_far(patch_group)

    def reduced(parts):
        arrived = {step: far(parts[step], step) for step in AROUND}
        return added(parts[0], [arrived[step] for step in range(1, SIDE)]).astype(jnp.bfloat16)

    *parts, kept = attend(0, lists, patch_pieces, kv_zero, gains, (w_query[0], theirs), outs)
    kv_second, _ = lax.optimization_barrier((kv_second, kept))
    arrived = to_patch(kv_second, (2, 6, 1, 7))
    arrived |= to_patch(kv_second, (4, 3, 5))
    same = jnp.stack([kv_second] + [arrived[step] for step in range(1, patch_count)])
    kv_one = (same, swapped(same))

    total = reduced(parts)
    first, *others = all_near(total)
    after_zero = (kept.astype(jnp.float32) + added(first, others)).astype(jnp.bfloat16)

    pieces = all_far(after_zero)
    *parts, _ = attend(1, lists, pieces, kv_one, gains, (w_query[0], theirs), outs)
    total = reduced(parts)
    own_zero = lax.dynamic_index_in_dim(after_zero, near_at, 0, keepdims=False)
    own_total = lax.dynamic_index_in_dim(total, near_at, 0, keepdims=False)
    others = [
        near(lax.dynamic_index_in_dim(total, wrapped(near_at + step), 0, keepdims=False), step)
        for step in AROUND
    ]
    own_one = (own_zero.astype(jnp.float32) + added(own_total, others)).astype(jnp.bfloat16)

    arrived = swapped(jnp.where(core == 0, own_one, own_zero))
    upper = jnp.where(core == 0, own_zero, arrived)
    lower = jnp.where(core == 0, arrived, own_one)
    return jnp.concatenate([upper, lower], axis=0)[None]


def solution(mesh):
    in_specs = (
        P("patch", "obs"),
        P("patch", "obs"),
        P("patch", None),
        P("patch"),
        P("patch", None),
        P("pipe", None, "obs"),
        P("pipe", None, "obs"),
        P("pipe", None, "obs"),
        P("pipe", "obs", None),
        P("pipe", None),
        P("pipe", None),
    )
    out_specs = P("pipe", "patch", "obs")
    return jax.shard_map(
        on_device, mesh=mesh, in_specs=in_specs, out_specs=out_specs, check_vma=False
    )
```
